128 devices in a mesh: gx: 16 (over y, x), gy: 8 (over z, core).
Axes of the slice: x: 4, y: 4, z: 4, core: 2. Of those that a mesh axis runs over, the one named last changes fastest.
Arguments:
- prior_member_matrix: float32 [8, 256, 256, 128], P(None, 'gx', 'gy'), may hold values from -6 to 6
- east_speed: float32 [4, 256, 256], P(None, 'gx', 'gy'), may hold values from -0.3 to 0.3
- north_speed: float32 [4, 256, 256], P(None, 'gx', 'gy'), may hold values from -0.3 to 0.3
- diffusion: float32 [4, 256, 256], P(None, 'gx', 'gy'), may hold values from 0.1 to 0.22
- obs_column: int32 [1024, 2], replicated, may hold values from 0 to 255, as said below
- obs_comp: int32 [1024], replicated, may hold values from 0 to 7
- observation_reach: int32 [1024], replicated, may hold values from 0 to 3
- obs_owner: int32 [1024], replicated, may hold values from 0 to 15, as said below
- obs_order: int32 [1024], replicated, may hold values from 0 to 1023, each once
- obs_value: float32 [16, 8, 32], P('gx', 'gy'), may hold values from -6 to 6
- obs_error: float32 [16, 8, 32], P('gx', 'gy'), may hold values from 0.3 to 3
Outputs:
- analysis: float32 [8, 256, 256, 128], P(None, 'gx', 'gy')
The draws below stay inside these ranges and needn't reach their ends.
Inputs may be any that keep to these rules, and one draw needn't show every extreme that they name: `obs_column`: tile t = (8 tx + ty) holds observations 8 t to 8 (t + 1) - 1; each entry is a (longitude, latitude) column inside that tile. `obs_owner`: the owner lies in the observation's latitude tile; one tile's observations reach one owner at most 2 times, and exactly 2 times for some owner of every tile.
All inputs are finite; a program needn't handle non-finite values.
Results may differ from the reference program's by a relative error of at most 0.0001.
Values sent between devices are 32-bit elements; how exact they have to be, the bound alone decides.
No kernel may reach another device: no remote copies, remote signals or barrier semaphores. Data moves between devices by JAX's collectives and lax.ppermute only.
A program may use at most 64 MiB of HBM per device.

```python
import math
import jax
import jax.numpy as jnp
from jax import lax

MEM = 128
LEV = 4
FSTEPS = 2
PANEL = 256
CX = 16
CY = 32
OBS_DEV = 8
COMP = 8
NX = 256
NY = 256
TILES_X = 16
TILES_Y = 8
CAP = 2
SLOTS = 32
NOBS = 1024
PANELS = 4
N_GX = 16
N_GY = 8


def obs_layout(key):
    tiles_x = NX // CX
    tiles_y = NY // CY
    sources = tiles_x * tiles_y
    sub_keys = jax.random.split(key, 4)
    source = jnp.arange(NOBS, dtype=jnp.int32) // OBS_DEV
    tile_x = source // tiles_y
    tile_y = source % tiles_y
    local_x = jax.random.randint(sub_keys[0], (NOBS,), 0, CX, dtype=jnp.int32)
    local_y = jax.random.randint(sub_keys[1], (NOBS,), 0, CY, dtype=jnp.int32)
    columns = jnp.stack([tile_x * CX + local_x, tile_y * CY + local_y], axis=1).astype(jnp.int32)
    slot_total = tiles_x * CAP
    favoured = jax.random.randint(sub_keys[2], (sources,), 0, tiles_x, dtype=jnp.int32)
    noise = jax.random.randint(sub_keys[3], (sources, slot_total), 0, 65536, dtype=jnp.int32)
    slot_ids = jnp.arange(slot_total, dtype=jnp.int32)
    target = slot_ids // CAP
    scores = noise * slot_total + slot_ids[None, :]
    scores = jnp.where(target[None, :] == favoured[:, None], slot_ids[None, :] - slot_total, scores)
    picked = jnp.argsort(scores, axis=1, stable=True)[:, :OBS_DEV].astype(jnp.int32)
    owners = (picked // CAP).reshape(NOBS).astype(jnp.int32)
    return (columns, owners)


def draw_obs_column(key, part):
    return obs_layout(jax.random.fold_in(key, 11))[0]


def draw_obs_owner(key, part):
    return obs_layout(jax.random.fold_in(key, 11))[1]


def with_ends(entries, rng, smallest, high):
    dims = entries.shape
    index_at = [jax.random.randint(jax.random.fold_in(rng, axis), (), 0, dims[axis]) for axis in range(len(dims))]
    entries = entries.at[tuple(index_at)].set(smallest)
    longest = dims.index(max(dims))
    index_at[longest] = (index_at[longest] + 1) % dims[longest]
    return entries.at[tuple(index_at)].set(high)


def shard_levels(stream_key, shape, pieces, low, top_value):
    def one(dim, shards_of):
        heights = jax.random.uniform(jax.random.fold_in(jax.random.fold_in(stream_key, 6), dim), (shards_of,), jnp.float32, low / len(pieces), top_value / len(pieces))
        return jnp.repeat(jnp.exp(heights), shape[dim] // shards_of).reshape((-1,) + (1,) * (len(shape) - dim - 1))

    loudness = one(*pieces[0])
    for cut in pieces[1:]:
        loudness = loudness * one(*cut)
    return loudness


def gaussian(rng, shape, deviation, most, pieces=(), held_as=jnp.bfloat16):
    array = deviation * jax.random.normal(rng, shape, jnp.float32)
    if pieces:
        array = array * shard_levels(rng, shape, pieces, -0.22, 0.18)
    return jnp.clip(array, -most, most).astype(held_as)


def setup_inputs(seed: int = 0) -> dict:
    splits = jax.random.split(jax.random.key(seed), 12)
    return {
        "prior_member_matrix": gaussian(splits[0], (COMP, NX, NY, MEM), 1.0, 6.0, ((1, 16), (2, 8)), jnp.float32),
        "east_speed": jnp.clip(jax.random.uniform(splits[1], (LEV, NX, NY), jnp.float32, -0.3, 0.3) * shard_levels(splits[1], (LEV, NX, NY), ((1, 16), (2, 8)), -0.4, 0.0), -0.3, 0.3),
        "north_speed": jnp.clip(jax.random.uniform(splits[2], (LEV, NX, NY), jnp.float32, -0.3, 0.3) * shard_levels(splits[2], (LEV, NX, NY), ((1, 16), (2, 8)), -0.4, 0.0), -0.3, 0.3),
        "diffusion": jnp.clip(0.1 + 0.12 * jax.random.uniform(splits[3], (LEV, NX, NY), jnp.float32) ** shard_levels(splits[3], (LEV, NX, NY), ((1, 16), (2, 8)), -0.2, 0.2), 0.1, 0.22),
        "obs_column": draw_obs_column(jax.random.fold_in(splits[11], 71), 0),
        "obs_comp": with_ends(jax.random.randint(splits[5], (NOBS,), 0, COMP), jax.random.fold_in(splits[5], 1), 0, COMP - 1).astype(jnp.int32),
        "observation_reach": with_ends(jax.random.randint(splits[6], (NOBS,), 0, LEV), jax.random.fold_in(splits[6], 1), 0, LEV - 1).astype(jnp.int32),
        "obs_owner": draw_obs_owner(jax.random.fold_in(splits[11], 71), 0),
        "obs_order": jax.random.permutation(splits[8], NOBS).astype(jnp.int32),
        "obs_value": gaussian(splits[9], (TILES_X, TILES_Y, SLOTS), 1.5, 6.0, ((0, 16), (1, 8)), jnp.float32),
        "obs_error": jnp.clip(jnp.exp(math.log(3.0) - 2.3025851 * jax.random.uniform(splits[10], (TILES_X, TILES_Y, SLOTS), jnp.float32) ** shard_levels(splits[10], (TILES_X, TILES_Y, SLOTS), ((0, 16), (1, 8)), -0.2, 0.2)), 0.3, 3.0),
    }


PRECISE = lax.Precision.HIGHEST

def slot_rank(tile_x, tile_y, owner, tiles_x, tiles_y):
    total_obs = owner.shape[0]
    keyed = (tile_x * tiles_y + tile_y) * tiles_x + owner
    sort_order = jnp.argsort(keyed, stable=True).astype(jnp.int32)
    sorted_keys = keyed[sort_order]
    places = jnp.arange(total_obs, dtype=jnp.int32)
    segment_beginning = jnp.concatenate([jnp.ones((1,), dtype=bool), sorted_keys[1:] != sorted_keys[:-1]])
    starts = lax.cummax(jnp.where(segment_beginning, places, 0), axis=0)
    ranked = places - starts
    inverse_order = jnp.argsort(sort_order).astype(jnp.int32)
    return ranked[inverse_order]

def horizontal(first_x, first_y, second_x, second_y, span_x, span_y, total_x):
    wrapped = (first_x - second_x) % total_x
    dist_x = jnp.minimum(wrapped, total_x - wrapped).astype(jnp.float32)
    dist_y = (first_y - second_y).astype(jnp.float32)
    radius_sq = (dist_x / span_x) ** 2 + (dist_y / span_y) ** 2
    return jnp.maximum(0.0, 1.0 - radius_sq) ** 2

def vertical(first_level, second_level, reach):
    level_gap = jnp.abs(first_level - second_level).astype(jnp.float32)
    return jnp.maximum(0.0, 1.0 - level_gap / (reach.astype(jnp.float32) + 1.0))

def panel_terms(priors, values, errors):
    members = priors.shape[1]
    centre = lax.optimization_barrier(jnp.mean(priors, axis=1))
    spread = priors - centre[:, None]
    variance = lax.optimization_barrier(jnp.sum(spread * spread, axis=1)) / (members - 1)
    inverse = 1.0 / (variance + errors)
    damping = 1.0 / (1.0 + jnp.sqrt(errors * inverse))
    return (spread, (values - centre) * inverse, damping * inverse)

def regress(row_block, weight, spread, mean_gain, shrink):
    members = row_block.shape[1]
    centre = lax.optimization_barrier(jnp.mean(row_block, axis=1, keepdims=True))
    anomaly = row_block - centre
    covariance = jnp.dot(anomaly, spread.T, precision=PRECISE, preferred_element_type=jnp.float32) / (members - 1)
    weighted = weight * covariance
    centre = centre + jnp.dot(weighted, mean_gain[:, None], precision=PRECISE, preferred_element_type=jnp.float32)
    anomaly = anomaly - jnp.dot(weighted * shrink[None, :], spread, precision=PRECISE, preferred_element_type=jnp.float32)
    return centre + anomaly

def advance(model_mesh_values, east_vel, north_vel, diff_coef):
    east_side = jnp.roll(model_mesh_values, -1, axis=0)
    west_side = jnp.roll(model_mesh_values, 1, axis=0)
    padded = jnp.pad(model_mesh_values, ((0, 0), (1, 1), (0, 0)))
    north_side = padded[:, 2:]
    south_side = padded[:, :-2]
    spread_term = diff_coef * (east_side + west_side + north_side + south_side - 4.0 * model_mesh_values)
    carry_term = 0.5 * (east_vel * (east_side - west_side) + north_vel * (north_side - south_side))
    return model_mesh_values + spread_term - carry_term

def reference(prior_member_matrix, east_speed, north_speed, diffusion, obs_column, obs_comp, observation_reach, obs_owner, obs_order, obs_value, obs_error):
    per_level = COMP // LEV

    def predicted_entry(compact_storage):
        model_mesh_values, east_vel, north_vel, diff_coef = compact_storage
        for substep in range(FSTEPS):
            model_mesh_values = advance(model_mesh_values, east_vel[..., None], north_vel[..., None], diff_coef[..., None])
        return model_mesh_values
    flow_velocities = [jnp.repeat(table, per_level, axis=0) for table in (east_speed, north_speed, diffusion)]
    model_mesh_values = lax.map(predicted_entry, (prior_member_matrix, flow_velocities[0], flow_velocities[1], flow_velocities[2]))
    col_x = obs_column[:, 0]
    col_y = obs_column[:, 1]
    tile_x = col_x // CX
    tile_y = col_y // CY
    ranked_slot = slot_rank(tile_x, tile_y, obs_owner, N_GX, N_GY)
    slot_place = tile_x * CAP + ranked_slot
    values = obs_value[obs_owner, tile_y, slot_place]
    errors = obs_error[obs_owner, tile_y, slot_place]
    obs_level = obs_comp // per_level
    grid_x = jnp.repeat(jnp.arange(NX, dtype=jnp.int32), NY)
    grid_y = jnp.tile(jnp.arange(NY, dtype=jnp.int32), NX)
    comp_level = jnp.arange(COMP, dtype=jnp.int32) // per_level
    for panel_num in range(PANELS):
        panel_index_list = obs_order[panel_num * PANEL:(panel_num + 1) * PANEL]
        priors = model_mesh_values[obs_comp[panel_index_list], col_x[panel_index_list], col_y[panel_index_list]]
        spread, mean_gain, shrink = panel_terms(priors, values[panel_index_list], errors[panel_index_list])
        flat_weight = horizontal(grid_x[:, None], grid_y[:, None], col_x[panel_index_list][None, :], col_y[panel_index_list][None, :], 3.0 * CX, 3.0 * CY, NX)
        levels = vertical(comp_level[:, None], obs_level[panel_index_list][None, :], observation_reach[panel_index_list][None, :])

        def update(compact_storage):
            component_block, level_row = compact_storage
            row_block = regress(component_block.reshape(NX * NY, MEM), flat_weight * level_row[None, :], spread, mean_gain, shrink)
            return row_block.reshape(NX, NY, MEM)
        model_mesh_values = lax.map(update, (model_mesh_values, levels))
    return model_mesh_values
```

```python
import jax
import jax.numpy as jnp
from jax import lax
from jax.experimental import pallas as pl
from jax.experimental.pallas import tpu as pltpu
from jax.sharding import PartitionSpec as P

FSTEPS = 2
PANEL = 256
PANELS = 4
NOBS = 1024
COMP = 8
CX = 16
CY = 32
MEM = 128
BLOCK = CX * CY
F32 = jnp.float32
BF16 = jnp.bfloat16
NT = (((1,), (1,)), ((), ()))
NN = (((1,), (0,)), ((), ()))


def with_halo(cells, sides, width, closed):
    for axis, dim in sides:
        count = lax.axis_size(axis)
        ends = count if closed else count - 1
        head = lax.slice_in_dim(cells, 0, width, axis=dim)
        tail = lax.slice_in_dim(cells, cells.shape[dim] - width, cells.shape[dim], axis=dim)
        cells = jnp.concatenate(
            [
                lax.ppermute(tail, axis, [(i, (i + 1) % count) for i in range(ends)]),
                cells,
                lax.ppermute(head, axis, [((i + 1) % count, i) for i in range(ends)]),
            ],
            axis=dim,
        )
    return cells


def dot(left, right, dims=NN):
    return lax.dot_general(left, right, dims, preferred_element_type=F32)


def halves(full):
    high = full.astype(BF16)
    low = (full - high.astype(F32)).astype(BF16)
    return high, low


def as_columns(row):
    return jnp.transpose(jnp.broadcast_to(row, (128, row.shape[1])))


def plan_kernel(pos, table, perm, obs_weight, select, slots, source, place, counts):
    here_x = pos[0]
    here_y = pos[1]
    owner = table[4:5, :]
    lane = lax.broadcasted_iota(jnp.int32, (1, NOBS), 1)
    within = lane & 7
    rank = jnp.zeros((1, NOBS), jnp.int32)
    for gap in range(1, 8):
        same = (within >= gap) & (pltpu.roll(owner, gap, 1) == owner)
        rank = rank + same.astype(jnp.int32)
    place_row = (lane >> 6) * 2 + rank
    source_row = owner * 8 + ((lane >> 3) & 7)
    facts = jnp.concatenate(
        [table[0:4, :], place_row, source_row, jnp.zeros((2, NOBS), jnp.int32)], axis=0
    ).astype(F32)
    order = as_columns(table[5:6, :].astype(F32))
    lanes = lax.broadcasted_iota(jnp.int32, (NOBS, 128), 1).astype(F32)
    for part in range(NOBS // 128):
        hit = order == lanes + float(128 * part)
        perm[:, part * 128 : (part + 1) * 128] = jnp.where(hit, 1.0, 0.0).astype(BF16)
    ordered = dot(facts.astype(BF16), perm[...], NT)

    col_x = as_columns(ordered[0:1])
    col_y = as_columns(ordered[1:2])
    col_l = as_columns(ordered[2:3])
    place[...] = as_columns(ordered[4:5])
    col_s = as_columns(ordered[5:6])
    source[...] = jnp.where(col_s == lanes, 1.0, 0.0).astype(BF16)
    inverse = 1.0 / (ordered[3:4] + 1.0)
    first = 0
    for panel in range(PANELS - 1):
        begin = (panel + 1) * PANEL
        rows = NOBS - begin
        for part in range(PANEL // 128):
            cols = slice(panel * PANEL + part * 128, panel * PANEL + (part + 1) * 128)
            gap_x = jnp.abs(col_x[begin:] - ordered[0:1, cols])
            gap_x = jnp.minimum(gap_x, 256.0 - gap_x)
            gap_y = col_y[begin:] - ordered[1:2, cols]
            near = jnp.maximum(0.0, 1.0 - (gap_x * gap_x * (1.0 / 2304.0) + gap_y * gap_y * (1.0 / 9216.0)))
            gap_l = jnp.abs(col_l[begin:] - ordered[2:3, cols])
            level = jnp.maximum(0.0, 1.0 - gap_l * inverse[:, cols])
            obs_weight[first : first + rows, part * 128 : (part + 1) * 128] = (
                near * near * level * (1.0 / (MEM - 1))
            )
        first += rows

    whole = ordered.astype(jnp.int32)
    off_x = (whole[0:1] - here_x * CX) & 255
    far_x = jnp.where(off_x < CX, 0, jnp.minimum(off_x - (CX - 1), 256 - off_x))
    off_y = whole[1:2] - here_y * CY
    far_y = jnp.maximum(0, jnp.maximum(-off_y, off_y - (CY - 1)))
    reached = jnp.where(4 * far_x * far_x + far_y * far_y < 9216, 1.0, 0.0)
    before = lax.broadcasted_iota(jnp.int32, (PANEL, PANEL), 0) < lax.broadcasted_iota(
        jnp.int32, (PANEL, PANEL), 1
    )
    before = jnp.where(before, 1.0, 0.0).astype(BF16)
    slot = lax.broadcasted_iota(jnp.int32, (PANEL, PANEL), 0).astype(F32)
    for panel in range(PANELS):
        cols = slice(panel * PANEL, (panel + 1) * PANEL)
        mask = reached[:, cols]
        ranks = dot(jnp.broadcast_to(mask, (8, PANEL)).astype(BF16), before)[0:1]
        chosen = jnp.where((slot == ranks) & (mask > 0.0), 1.0, 0.0).astype(BF16)
        select[panel] = chosen
        packed = dot(ordered[:, cols].astype(BF16), chosen, NT)
        slots[panel] = jnp.concatenate(
            [packed[0:3], 1.0 / (packed[3:4] + 1.0), packed[4:8]], axis=0
        )
        counts[panel] = jnp.sum(mask).astype(jnp.int32)


def analysis_kernel(
    pos, counts, priors, given, state, perm, obs_weight, select, slots, source, place,
    out, rows, near, left, right,
):
    here_x = pos[0]
    here_y = pos[1]
    high, low = halves(priors[...])
    both = jnp.concatenate([high, low], axis=1)
    for panel in range(PANELS):
        span = slice(panel * PANEL, (panel + 1) * PANEL)
        moved = dot(perm[span, :], both)
        rows[span, :] = moved[:, :MEM] + moved[:, MEM:]
    v_high = given[...].astype(BF16)
    rest = given[...] - v_high.astype(F32)
    v_mid = rest.astype(BF16)
    v_low = (rest - v_mid.astype(F32)).astype(BF16)
    v_all = jnp.concatenate([v_high, v_mid, v_low], axis=1)
    lanes = lax.broadcasted_iota(jnp.int32, (PANEL, 128), 1).astype(F32)

    first = 0
    for panel in range(PANELS):
        span = slice(panel * PANEL, (panel + 1) * PANEL)
        held = dot(source[span, :], v_all)
        held = held[:, :128] + held[:, 128:256] + held[:, 256:]
        here = place[span, :]
        value = jnp.sum(jnp.where(lanes == here, held, 0.0), axis=1, keepdims=True)
        error = jnp.sum(jnp.where(lanes == here + 32.0, held, 0.0), axis=1, keepdims=True)
        prior = rows[span, :]
        centre = jnp.sum(prior, axis=1, keepdims=True) * (1.0 / MEM)
        spread = prior - centre
        variance = jnp.sum(spread * spread, axis=1, keepdims=True) / (MEM - 1)
        inverse = 1.0 / (variance + error)
        gain = (value - centre) * inverse
        shrink = inverse / (1.0 + jnp.sqrt(error * inverse))
        change = gain - shrink * spread
        q_high, q_low = halves(spread)
        h_high, h_low = halves(change)
        if panel < PANELS - 1:
            begin = (panel + 1) * PANEL
            count = NOBS - begin
            later = rows[begin:, :]
            l_high, l_low = halves(later - jnp.sum(later, axis=1, keepdims=True) * (1.0 / MEM))
            q_both = jnp.concatenate(
                [jnp.concatenate([q_high, q_high], axis=1), jnp.concatenate([q_low, q_low], axis=1)], axis=0
            )
            cov = dot(jnp.concatenate([l_high, l_low], axis=1), q_both, NT)
            local = (cov[:, :PANEL] + cov[:, PANEL:]) * obs_weight[first : first + count, :]
            g_high, g_low = halves(local)
            h_both = jnp.concatenate([h_high, h_low], axis=1)
            step = dot(g_high, h_both) + dot(g_low, h_both)
            rows[begin:, :] = later + (step[:, :MEM] + step[:, MEM:])
            first += count
        packed = dot(select[panel], jnp.concatenate([q_high, q_low, h_high, h_low], axis=1)).astype(BF16)
        for part in range(2):
            half = packed[part * 128 : (part + 1) * 128]
            q_h, q_l, h_h, h_l = (half[:, i * MEM : (i + 1) * MEM] for i in range(4))
            left[panel, part] = jnp.concatenate(
                [jnp.concatenate([q_h, q_h], axis=1), jnp.concatenate([q_l, q_l], axis=1)], axis=0
            )
            h_row = jnp.concatenate([h_h, h_l], axis=1)
            right[panel, part] = jnp.concatenate([h_row, h_row], axis=0)
        fact = slots[panel]
        step_x = lax.broadcasted_iota(jnp.int32, (CX, PANEL), 0) + here_x * CX
        gap_x = jnp.abs(step_x.astype(F32) - fact[0:1])
        gap_x = jnp.minimum(gap_x, 256.0 - gap_x)
        part_x = 1.0 - gap_x * gap_x * (1.0 / 2304.0)
        step_y = lax.broadcasted_iota(jnp.int32, (CY, PANEL), 0) + here_y * CY
        gap_y = step_y.astype(F32) - fact[1:2]
        part_y = gap_y * gap_y * (1.0 / 9216.0)
        for col in range(CX):
            close = jnp.maximum(0.0, part_x[col : col + 1] - part_y)
            near[panel, col * CY : (col + 1) * CY, :] = close * close * (1.0 / (MEM - 1))

    @pl.loop(0, COMP)
    def _(comp):
        level = (comp // 2).astype(F32)
        at = pl.ds(pl.multiple_of(comp * BLOCK, BLOCK), BLOCK)
        block = state[at, :]
        mean = jnp.sum(block, axis=1, keepdims=True) * (1.0 / MEM)
        out[at, :] = block - mean
        for panel in range(PANELS):
            fact = slots[panel]
            level_weight = jnp.maximum(0.0, 1.0 - jnp.abs(fact[2:3] - level) * fact[3:4])

            def local_step(both, part):
                cov = dot(both, left[panel, part], NT)
                cols = slice(part * 128, (part + 1) * 128)
                local = (cov[:, :128] + cov[:, 128:]) * (near[panel, :, cols] * level_weight[:, cols])
                g_high, g_low = halves(local)
                step = dot(jnp.concatenate([g_high, g_low], axis=1), right[panel, part])
                return step[:, :MEM] + step[:, MEM:]

            old = out[at, :]
            old_high, old_low = halves(old)
            old_both = jnp.concatenate([old_high, old_low], axis=1)
            out[at, :] = old + local_step(old_both, 0)

            @pl.when(counts[panel] > 128)
            def _():
                out[at, :] = out[at, :] + local_step(old_both, 1)
        out[at, :] = out[at, :] + mean


def vmem():
    return pl.BlockSpec(memory_space=pltpu.VMEM)


def smem():
    return pl.BlockSpec(memory_space=pltpu.SMEM)


def plan(pos, table):
    shapes = (
        jax.ShapeDtypeStruct((NOBS, NOBS), BF16),
        jax.ShapeDtypeStruct((6 * PANEL, PANEL), F32),
        jax.ShapeDtypeStruct((PANELS, PANEL, PANEL), BF16),
        jax.ShapeDtypeStruct((PANELS, 8, PANEL), F32),
        jax.ShapeDtypeStruct((NOBS, 128), BF16),
        jax.ShapeDtypeStruct((NOBS, 128), F32),
        jax.ShapeDtypeStruct((PANELS,), jnp.int32),
    )
    return pl.pallas_call(
        plan_kernel,
        out_shape=shapes,
        in_specs=[smem(), vmem()],
        out_specs=[vmem()] * 6 + [smem()],
        name="plan",
    )(pos, table)


def analyse(pos, counts, priors, given, state, *planned):
    return pl.pallas_call(
        analysis_kernel,
        out_shape=jax.ShapeDtypeStruct(state.shape, F32),
        in_specs=[smem(), smem()] + [vmem()] * (3 + len(planned)),
        out_specs=vmem(),
        scratch_shapes=[
            pltpu.VMEM((NOBS, MEM), F32),
            pltpu.VMEM((PANELS, BLOCK, PANEL), F32),
            pltpu.VMEM((PANELS, 2, PANEL, PANEL), BF16),
            pltpu.VMEM((PANELS, 2, PANEL, PANEL), BF16),
        ],
        compiler_params=pltpu.CompilerParams(vmem_limit_bytes=48 << 20),
        name="analyse",
    )(pos, counts, priors, given, state, *planned)


def shards(
    prior_member_matrix,
    east_speed,
    north_speed,
    diffusion,
    obs_column,
    obs_comp,
    observation_reach,
    obs_owner,
    obs_order,
    obs_value,
    obs_error,
):
    comps, zonal_extent, width_y, members = prior_member_matrix.shape
    per_level = comps // east_speed.shape[0]
    here_x = lax.axis_index("gx")
    here_y = lax.axis_index("gy")
    pos = jnp.stack([here_x, here_y]).astype(jnp.int32)
    zero = jnp.zeros_like(obs_comp)
    table = jnp.stack(
        [
            obs_column[:, 0],
            obs_column[:, 1],
            obs_comp // per_level,
            observation_reach,
            obs_owner,
            obs_order,
            zero,
            zero,
        ]
    )
    perm, obs_weight, select, slots, source, place, counts = plan(pos, table)

    east_vel = jnp.repeat(east_speed, per_level, axis=0)[..., None]
    north_vel = jnp.repeat(north_speed, per_level, axis=0)[..., None]
    diff_coef = jnp.repeat(diffusion, per_level, axis=0)[..., None]
    cells = prior_member_matrix
    for substep in range(FSTEPS):
        rim_wide = with_halo(cells, (("gx", 1),), 1, True)
        rim_tall = with_halo(cells, (("gy", 2),), 1, False)
        east_side = rim_wide[:, 2:]
        west_side = rim_wide[:, :-2]
        north_side = rim_tall[:, :, 2:]
        south_side = rim_tall[:, :, :-2]
        spread_term = diff_coef * (east_side + west_side + north_side + south_side - 4.0 * cells)
        carry_term = 0.5 * (
            east_vel * (east_side - west_side) + north_vel * (north_side - south_side)
        )
        cells = cells + spread_term - carry_term
    state = cells.reshape(comps * zonal_extent * width_y, members)

    begin = (here_x * lax.axis_size("gy") + here_y) * 8
    mine = lax.dynamic_slice(obs_column, (begin, 0), (8, 2))
    mine_comp = lax.dynamic_slice(obs_comp, (begin,), (8,))
    element = (mine_comp * zonal_extent + mine[:, 0] - here_x * zonal_extent) * width_y + (
        mine[:, 1] - here_y * width_y
    )
    held = jnp.concatenate([obs_value.reshape(1, -1), obs_error.reshape(1, -1)], axis=1)
    held = jnp.pad(held, ((0, 0), (0, members - held.shape[1])))
    bundle = jnp.concatenate([state[element], held], axis=0)
    bundle = jnp.broadcast_to(bundle.reshape(1, 9, 1, members), (128, 9, 1, members))
    arrived = lax.all_to_all(bundle, ("gx", "gy"), 0, 0, tiled=True)
    priors = arrived[:, :8].reshape(NOBS, members)
    given = arrived[:, 8].reshape(128, members)
    result = analyse(
        pos, counts, priors, given, state, perm, obs_weight, select, slots, source, place
    )
    return result.reshape(comps, zonal_extent, width_y, members)


def solution(mesh):
    return jax.shard_map(
        shards,
        mesh=mesh,
        in_specs=(
            P(None, "gx", "gy", None),
            P(None, "gx", "gy"),
            P(None, "gx", "gy"),
            P(None, "gx", "gy"),
            P(),
            P(),
            P(),
            P(),
            P(),
            P("gx", "gy", None),
            P("gx", "gy", None),
        ),
        out_specs=P(None, "gx", "gy", None),
        check_vma=False,
    )
```

```python
import jax
import jax.numpy as jnp
from jax import lax
from jax.experimental import pallas as pl
from jax.experimental.pallas import tpu as pltpu
from jax.sharding import PartitionSpec as P

FSTEPS = 2
PANEL = 256
PANELS = 4
NOBS = 1024
COMP = 8
CX = 16
CY = 32
MEM = 128
BLOCK = CX * CY
F32 = jnp.float32
BF16 = jnp.bfloat16
NT = (((1,), (1,)), ((), ()))
NN = (((1,), (0,)), ((), ()))


def dot(left, right, dims=NN):
    return lax.dot_general(left, right, dims, preferred_element_type=F32)


def halves(full):
    high = full.astype(BF16)
    low = (full - high.astype(F32)).astype(BF16)
    return high, low


def as_columns(row):
    return jnp.transpose(jnp.broadcast_to(row, (128, row.shape[1])))


def plan_kernel(pos, table, perm, obs_weight, select, slots, source, place, counts):
    here_x = pos[0]
    here_y = pos[1]
    owner = table[4:5, :]
    lane = lax.broadcasted_iota(jnp.int32, (1, NOBS), 1)
    within = lane & 7
    rank = jnp.zeros((1, NOBS), jnp.int32)
    for gap in range(1, 8):
        same = (within >= gap) & (pltpu.roll(owner, gap, 1) == owner)
        rank = rank + same.astype(jnp.int32)
    place_row = (lane >> 6) * 2 + rank
    source_row = owner * 8 + ((lane >> 3) & 7)
    facts = jnp.concatenate(
        [table[0:4, :], place_row, source_row, jnp.zeros((2, NOBS), jnp.int32)], axis=0
    ).astype(F32)
    order = as_columns(table[5:6, :].astype(F32))
    lanes = lax.broadcasted_iota(jnp.int32, (NOBS, 128), 1).astype(F32)
    for part in range(NOBS // 128):
        hit = order == lanes + float(128 * part)
        perm[:, part * 128 : (part + 1) * 128] = jnp.where(hit, 1.0, 0.0).astype(BF16)
    ordered = dot(facts.astype(BF16), perm[...], NT)

    col_x = as_columns(ordered[0:1])
    col_y = as_columns(ordered[1:2])
    col_l = as_columns(ordered[2:3])
    place[...] = as_columns(ordered[4:5])
    col_s = as_columns(ordered[5:6])
    source[...] = jnp.where(col_s == lanes, 1.0, 0.0).astype(BF16)
    inverse = 1.0 / (ordered[3:4] + 1.0)
    first = 0
    for panel in range(PANELS - 1):
        begin = (panel + 1) * PANEL
        rows = NOBS - begin
        for part in range(PANEL // 128):
            cols = slice(panel * PANEL + part * 128, panel * PANEL + (part + 1) * 128)
            gap_x = jnp.abs(col_x[begin:] - ordered[0:1, cols])
            gap_x = jnp.minimum(gap_x, 256.0 - gap_x)
            gap_y = col_y[begin:] - ordered[1:2, cols]
            near = jnp.maximum(0.0, 1.0 - (gap_x * gap_x * (1.0 / 2304.0) + gap_y * gap_y * (1.0 / 9216.0)))
            gap_l = jnp.abs(col_l[begin:] - ordered[2:3, cols])
            level = jnp.maximum(0.0, 1.0 - gap_l * inverse[:, cols])
            obs_weight[first : first + rows, part * 128 : (part + 1) * 128] = (
                near * near * level * (1.0 / (MEM - 1))
            )
        first += rows

    whole = ordered.astype(jnp.int32)
    off_x = (whole[0:1] - here_x * CX) & 255
    far_x = jnp.where(off_x < CX, 0, jnp.minimum(off_x - (CX - 1), 256 - off_x))
    off_y = whole[1:2] - here_y * CY
    far_y = jnp.maximum(0, jnp.maximum(-off_y, off_y - (CY - 1)))
    reached = jnp.where(4 * far_x * far_x + far_y * far_y < 9216, 1.0, 0.0)
    before = lax.broadcasted_iota(jnp.int32, (PANEL, PANEL), 0) < lax.broadcasted_iota(
        jnp.int32, (PANEL, PANEL), 1
    )
    before = jnp.where(before, 1.0, 0.0).astype(BF16)
    slot = lax.broadcasted_iota(jnp.int32, (PANEL, PANEL), 0).astype(F32)
    for panel in range(PANELS):
        cols = slice(panel * PANEL, (panel + 1) * PANEL)
        mask = reached[:, cols]
        ranks = dot(jnp.broadcast_to(mask, (8, PANEL)).astype(BF16), before)[0:1]
        chosen = jnp.where((slot == ranks) & (mask > 0.0), 1.0, 0.0).astype(BF16)
        select[panel] = chosen
        packed = dot(ordered[:, cols].astype(BF16), chosen, NT)
        slots[panel] = jnp.concatenate(
            [packed[0:3], 1.0 / (packed[3:4] + 1.0), packed[4:8]], axis=0
        )
        counts[panel] = jnp.sum(mask).astype(jnp.int32)


def analysis_kernel(
    pos, counts, priors, given, state, perm, obs_weight, select, slots, source, place,
    out, rows, near, left, right,
):
    here_x = pos[0]
    here_y = pos[1]
    high, low = halves(priors[...])
    both = jnp.concatenate([high, low], axis=1)
    for panel in range(PANELS):
        span = slice(panel * PANEL, (panel + 1) * PANEL)
        moved = dot(perm[span, :], both)
        rows[span, :] = moved[:, :MEM] + moved[:, MEM:]
    v_high = given[...].astype(BF16)
    rest = given[...] - v_high.astype(F32)
    v_mid = rest.astype(BF16)
    v_low = (rest - v_mid.astype(F32)).astype(BF16)
    v_all = jnp.concatenate([v_high, v_mid, v_low], axis=1)
    lanes = lax.broadcasted_iota(jnp.int32, (PANEL, 128), 1).astype(F32)

    first = 0
    for panel in range(PANELS):
        span = slice(panel * PANEL, (panel + 1) * PANEL)
        held = dot(source[span, :], v_all)
        held = held[:, :128] + held[:, 128:256] + held[:, 256:]
        here = place[span, :]
        value = jnp.sum(jnp.where(lanes == here, held, 0.0), axis=1, keepdims=True)
        error = jnp.sum(jnp.where(lanes == here + 32.0, held, 0.0), axis=1, keepdims=True)
        prior = rows[span, :]
        centre = jnp.sum(prior, axis=1, keepdims=True) * (1.0 / MEM)
        spread = prior - centre
        variance = jnp.sum(spread * spread, axis=1, keepdims=True) / (MEM - 1)
        inverse = 1.0 / (variance + error)
        gain = (value - centre) * inverse
        shrink = inverse / (1.0 + jnp.sqrt(error * inverse))
        change = gain - shrink * spread
        q_high, q_low = halves(spread)
        h_high, h_low = halves(change)
        if panel < PANELS - 1:
            begin = (panel + 1) * PANEL
            count = NOBS - begin
            later = rows[begin:, :]
            l_high, l_low = halves(later - jnp.sum(later, axis=1, keepdims=True) * (1.0 / MEM))
            q_both = jnp.concatenate(
                [jnp.concatenate([q_high, q_high], axis=1), jnp.concatenate([q_low, q_low], axis=1)], axis=0
            )
            cov = dot(jnp.concatenate([l_high, l_low], axis=1), q_both, NT)
            local = (cov[:, :PANEL] + cov[:, PANEL:]) * obs_weight[first : first + count, :]
            g_high, g_low = halves(local)
            h_both = jnp.concatenate([h_high, h_low], axis=1)
            step = dot(g_high, h_both) + dot(g_low, h_both)
            rows[begin:, :] = later + (step[:, :MEM] + step[:, MEM:])
            first += count
        packed = dot(select[panel], jnp.concatenate([q_high, q_low, h_high, h_low], axis=1)).astype(BF16)
        for part in range(2):
            half = packed[part * 128 : (part + 1) * 128]
            q_h, q_l, h_h, h_l = (half[:, i * MEM : (i + 1) * MEM] for i in range(4))
            left[panel, part] = jnp.concatenate(
                [jnp.concatenate([q_h, q_h], axis=1), jnp.concatenate([q_l, q_l], axis=1)], axis=0
            )
            h_row = jnp.concatenate([h_h, h_l], axis=1)
            right[panel, part] = jnp.concatenate([h_row, h_row], axis=0)
        fact = slots[panel]
        step_x = lax.broadcasted_iota(jnp.int32, (CX, PANEL), 0) + here_x * CX
        gap_x = jnp.abs(step_x.astype(F32) - fact[0:1])
        gap_x = jnp.minimum(gap_x, 256.0 - gap_x)
        part_x = 1.0 - gap_x * gap_x * (1.0 / 2304.0)
        step_y = lax.broadcasted_iota(jnp.int32, (CY, PANEL), 0) + here_y * CY
        gap_y = step_y.astype(F32) - fact[1:2]
        part_y = gap_y * gap_y * (1.0 / 9216.0)
        for col in range(CX):
            close = jnp.maximum(0.0, part_x[col : col + 1] - part_y)
            near[panel, col * CY : (col + 1) * CY, :] = close * close * (1.0 / (MEM - 1))

    @pl.loop(0, COMP)
    def _(comp):
        level = (comp // 2).astype(F32)
        at = pl.ds(pl.multiple_of(comp * BLOCK, BLOCK), BLOCK)
        block = state[at, :]
        mean = jnp.sum(block, axis=1, keepdims=True) * (1.0 / MEM)
        out[at, :] = block - mean
        for panel in range(PANELS):
            fact = slots[panel]
            level_weight = jnp.maximum(0.0, 1.0 - jnp.abs(fact[2:3] - level) * fact[3:4])

            def local_step(both, part):
                cov = dot(both, left[panel, part], NT)
                cols = slice(part * 128, (part + 1) * 128)
                local = (cov[:, :128] + cov[:, 128:]) * (near[panel, :, cols] * level_weight[:, cols])
                g_high, g_low = halves(local)
                step = dot(jnp.concatenate([g_high, g_low], axis=1), right[panel, part])
                return step[:, :MEM] + step[:, MEM:]

            old = out[at, :]
            old_high, old_low = halves(old)
            old_both = jnp.concatenate([old_high, old_low], axis=1)
            out[at, :] = old + local_step(old_both, 0)

            @pl.when(counts[panel] > 128)
            def _():
                out[at, :] = out[at, :] + local_step(old_both, 1)
        out[at, :] = out[at, :] + mean


OFFSETS = (
    (0, 0), (-1, 0), (1, 0), (0, -1), (0, 1),
    (-1, -1), (-1, 1), (1, -1), (1, 1),
    (-2, 0), (2, 0), (0, -2), (0, 2),
)


def edge_kernel(pos, code, cells, east, north, diff, own, own_coef, to_east, to_west, to_north, to_south):
    here_x = pos[0]
    here_y = pos[1]
    coefs = (east, north, diff)

    def look(shift_x, shift_y, k):
        tile_x = (here_x + shift_x) & 15
        tile_y = jnp.clip(here_y + shift_y, 0, 7)
        word = code[(tile_x * 8 + tile_y) * 8 + k]
        return word & 15, (word >> 8) & 31, word >> 16

    def cell(comp, x, y):
        return cells[pl.ds((comp * CX + x) * CY + y, 1), :]

    def clip_x(x):
        return jnp.clip(x, 0, CX - 1)

    def clip_y(y):
        return jnp.clip(y, 0, CY - 1)

    for k in range(8):
        x, y, comp = look(0, 0, k)
        for index, (step_x, step_y) in enumerate(OFFSETS):
            at = index * 8 + k
            own[at : at + 1, :] = cell(comp, clip_x(x + step_x), clip_y(y + step_y))
        for step_x in (-1, 0, 1):
            for c in range(3):
                at = (c * 3 + step_x + 1) * 8 + k
                own_coef[at : at + 1, 0:CY] = coefs[c][pl.ds((comp >> 1) * CX + clip_x(x + step_x), 1), :]
        for shift, target, edge in ((1, to_east, CX - 1), (-1, to_west, 0)):
            x, y, comp = look(shift, 0, k)
            for index, step_y in enumerate((-1, 0, 1)):
                at = index * 8 + k
                target[at : at + 1, :] = cell(comp, edge, clip_y(y + step_y))
            target[24 + k : 25 + k, :] = cell(comp, clip_x(x + shift * (CX - 2)), y)
            _, _, comp = look(shift, 1, k)
            target[32 + k : 33 + k, :] = cell(comp, edge, CY - 1)
            _, _, comp = look(shift, -1, k)
            target[40 + k : 41 + k, :] = cell(comp, edge, 0)
        for shift, target, edge in ((1, to_north, CY - 1), (-1, to_south, 0)):
            x, y, comp = look(0, shift, k)
            for index, step_x in enumerate((-1, 0, 1)):
                at = index * 8 + k
                target[at : at + 1, :] = cell(comp, clip_x(x + step_x), edge)
            target[24 + k : 25 + k, :] = cell(comp, x, clip_y(y + shift * (CY - 2)))
    for target, edge in ((to_east, CX - 1), (to_west, 0)):
        target[48:64, :] = jnp.zeros((16, MEM), F32)
        for c in range(3):
            for level in range(4):
                at = 48 + c * 4 + level
                target[at : at + 1, 0:CY] = coefs[c][level * CX + edge : level * CX + edge + 1, :]
    lanes = lax.broadcasted_iota(jnp.int32, (CX, MEM), 1)
    for target, edge in ((to_north, CY - 1), (to_south, 0)):
        table = jnp.zeros((CX, MEM), F32)
        for c in range(3):
            for level in range(4):
                line = coefs[c][level * CX : (level + 1) * CX, edge : edge + 1]
                table = jnp.where(lanes == c * 4 + level, line, table)
        target[32:48, :] = table


def obs_columns(pos, code):
    begin = (pos[0] * 8 + pos[1]) * 8
    row = lax.broadcasted_iota(jnp.int32, (8, MEM), 0)
    word = jnp.zeros((8, MEM), jnp.int32)
    for k in range(8):
        word = jnp.where(row == k, code[begin + k], word)
    return word & 15, (word >> 8) & 31, word >> 16


def corner_kernel(pos, code, base_north, base_south, from_west, from_east, to_north, to_south):
    row = lax.broadcasted_iota(jnp.int32, (8, MEM), 0)
    for shift, base, target, first in ((1, base_north, to_north, 32), (-1, base_south, to_south, 40)):
        tile_y = jnp.clip(pos[1] + shift, 0, 7)
        begin = (pos[0] * 8 + tile_y) * 8
        x = jnp.zeros((8, MEM), jnp.int32)
        for k in range(8):
            x = jnp.where(row == k, code[begin + k] & 15, x)
        target[...] = base[...]
        target[0:8, :] = jnp.where(x == 0, from_west[first : first + 8, :], base[0:8, :])
        target[16:24, :] = jnp.where(x == CX - 1, from_east[first : first + 8, :], base[16:24, :])


def prior_kernel(
    pos, code, own, own_coef, from_west, from_east, from_south, from_north, held, out, scratch
):
    x, y, comp = obs_columns(pos, code)
    level = comp >> 1
    west = x == 0
    east = x == CX - 1
    begin = (pos[0] * 8 + pos[1]) * 8
    for k in range(8):
        word = code[begin + k]
        here_l = word >> 17
        for c in range(3):
            at = c * 8 + k
            scratch[at : at + 1, :] = from_west[pl.ds(48 + c * 4 + here_l, 1), :]
            scratch[24 + at : 25 + at, :] = from_east[pl.ds(48 + c * 4 + here_l, 1), :]
        scratch[48 + k : 49 + k, :] = from_south[pl.ds(32 + (word & 15), 1), :]
        scratch[56 + k : 57 + k, :] = from_north[pl.ds(32 + (word & 15), 1), :]

    state = {}
    for index, (step_x, step_y) in enumerate(OFFSETS):
        value = own[index * 8 : index * 8 + 8, :]
        if step_x < 0:
            group = 3 if step_x == -2 else step_y + 1
            value = jnp.where(x + step_x < 0, from_west[group * 8 : group * 8 + 8, :], value)
        if step_x > 0:
            group = 3 if step_x == 2 else step_y + 1
            value = jnp.where(x + step_x >= CX, from_east[group * 8 : group * 8 + 8, :], value)
        if step_y < 0:
            group = 3 if step_y == -2 else step_x + 1
            value = jnp.where(y + step_y < 0, from_south[group * 8 : group * 8 + 8, :], value)
        if step_y > 0:
            group = 3 if step_y == 2 else step_x + 1
            value = jnp.where(y + step_y >= CY, from_north[group * 8 : group * 8 + 8, :], value)
        state[(step_x, step_y)] = value

    lanes = lax.broadcasted_iota(jnp.int32, (8, MEM), 1)
    at_y = lanes[:, :CY] - y[:, :CY]

    def pick(values, mask):
        return jnp.sum(jnp.where(mask, values, 0.0), axis=1, keepdims=True)

    def rows_of(c, step_x):
        at = (c * 3 + step_x + 1) * 8
        return own_coef[at : at + 8, 0:CY]

    def coefs_at(step_x, step_y):
        found = []
        for c in range(3):
            value = pick(rows_of(c, step_x), at_y == step_y)
            if step_x == -1:
                value = jnp.where(west[:, :1], pick(scratch[c * 8 : c * 8 + 8, 0:CY], at_y == 0), value)
            if step_x == 1:
                value = jnp.where(east[:, :1], pick(scratch[24 + c * 8 : 32 + c * 8, 0:CY], at_y == 0), value)
            mine = lanes == c * 4 + level
            if step_y == -1:
                value = jnp.where(y[:, :1] == 0, pick(scratch[48:56, :], mine), value)
            if step_y == 1:
                value = jnp.where(y[:, :1] == CY - 1, pick(scratch[56:64, :], mine), value)
            found.append(value)
        return found

    def advance(field, step_x, step_y):
        u, v, nu = coefs_at(step_x, step_y)
        mid = field[(step_x, step_y)]
        e = field[(step_x + 1, step_y)]
        w = field[(step_x - 1, step_y)]
        n = field[(step_x, step_y + 1)]
        s = field[(step_x, step_y - 1)]
        return mid + nu * (e + w + n + s - 4.0 * mid) - 0.5 * (u * (e - w) + v * (n - s))

    after = {key: advance(state, *key) for key in OFFSETS[:5]}
    out[0:8, :] = advance(after, 0, 0)
    out[8:9, :] = held[...]


def stencil(mid, e, w, n, s, u, v, nu):
    return mid + nu * (e + w + n + s - 4.0 * mid) - 0.5 * (u * (e - w) + v * (n - s))


def forecast_kernel(
    cells, east, north, diff, halo_w, halo_e, halo_s, halo_n, edge_w, edge_e, edge_s, edge_n,
    out, table, before, after,
):
    coefs = (east, north, diff)
    pad = jnp.zeros((128 - CX, CY), F32)
    fill = jnp.zeros((128, 128 - CY), F32)
    for c in range(3):
        for level in range(4):
            tile = coefs[c][level * CX : (level + 1) * CX, :]
            ends = jnp.concatenate(
                [
                    tile,
                    edge_w[48 + c * 4 + level : 49 + c * 4 + level, 0:CY],
                    edge_e[48 + c * 4 + level : 49 + c * 4 + level, 0:CY],
                    pad[: 128 - CX - 2],
                ],
                axis=0,
            )
            turned = jnp.transpose(jnp.concatenate([ends, fill], axis=1))
            table[level, c] = turned[0:CY, :]

    mid_rows = slice(8, 8 + CY)
    for level in range(4):
        for which in range(2):
            comp = level * 2 + which
            before[which, 2 : 2 + CX, mid_rows, :] = cells[comp]
            before[which, 0:2, mid_rows, :] = halo_w[comp]
            before[which, 2 + CX : 4 + CX, mid_rows, :] = halo_e[comp]
            before[which, 1 : 3 + CX, 7, :] = halo_s[comp, :, 1, :]
            before[which, 1 : 3 + CX, 8 + CY, :] = halo_n[comp, :, 0, :]
        for col in range(-1, CX + 1):
            lane = CX if col < 0 else (CX + 1 if col == CX else col)
            u, v, nu = (
                jnp.broadcast_to(table[level, c, :, lane : lane + 1], (CY, MEM)) for c in range(3)
            )
            at = col + 2
            for which in range(2):
                after[which, at, mid_rows, :] = stencil(
                    before[which, at, mid_rows, :],
                    before[which, at + 1, mid_rows, :],
                    before[which, at - 1, mid_rows, :],
                    before[which, at, 9 : 9 + CY, :],
                    before[which, at, 7 : 7 + CY, :],
                    u, v, nu,
                )
        for rim, edge, inner, outer, inside, target in (
            (halo_s, edge_s, 1, 0, 0, 7),
            (halo_n, edge_n, 0, 1, CY - 1, 8 + CY),
        ):
            u, v, nu = (
                jnp.broadcast_to(edge[32:48, c * 4 + level : c * 4 + level + 1], (CX, MEM))
                for c in range(3)
            )
            for which in range(2):
                comp = level * 2 + which
                mid = rim[comp, 1 : 1 + CX, inner, :]
                e = rim[comp, 2 : 2 + CX, inner, :]
                w = rim[comp, 0:CX, inner, :]
                far = rim[comp, 1 : 1 + CX, outer, :]
                close = cells[comp, :, inside, :]
                n, s = (close, far) if target == 7 else (far, close)
                after[which, 2 : 2 + CX, target, :] = stencil(mid, e, w, n, s, u, v, nu)
        for col in range(CX):
            u, v, nu = (
                jnp.broadcast_to(table[level, c, :, col : col + 1], (CY, MEM)) for c in range(3)
            )
            at = col + 2
            for which in range(2):
                out[level * 2 + which, col] = stencil(
                    after[which, at, mid_rows, :],
                    after[which, at + 1, mid_rows, :],
                    after[which, at - 1, mid_rows, :],
                    after[which, at, 9 : 9 + CY, :],
                    after[which, at, 7 : 7 + CY, :],
                    u, v, nu,
                )


def vmem():
    return pl.BlockSpec(memory_space=pltpu.VMEM)


def smem():
    return pl.BlockSpec(memory_space=pltpu.SMEM)


def plan(pos, table):
    shapes = (
        jax.ShapeDtypeStruct((NOBS, NOBS), BF16),
        jax.ShapeDtypeStruct((6 * PANEL, PANEL), F32),
        jax.ShapeDtypeStruct((PANELS, PANEL, PANEL), BF16),
        jax.ShapeDtypeStruct((PANELS, 8, PANEL), F32),
        jax.ShapeDtypeStruct((NOBS, 128), BF16),
        jax.ShapeDtypeStruct((NOBS, 128), F32),
        jax.ShapeDtypeStruct((PANELS,), jnp.int32),
    )
    return pl.pallas_call(
        plan_kernel,
        out_shape=shapes,
        in_specs=[smem(), vmem()],
        out_specs=[vmem()] * 6 + [smem()],
        name="plan",
    )(pos, table)


def analyse(pos, counts, priors, given, state, *planned):
    return pl.pallas_call(
        analysis_kernel,
        out_shape=jax.ShapeDtypeStruct(state.shape, F32),
        in_specs=[smem(), smem()] + [vmem()] * (3 + len(planned)),
        out_specs=vmem(),
        scratch_shapes=[
            pltpu.VMEM((NOBS, MEM), F32),
            pltpu.VMEM((PANELS, BLOCK, PANEL), F32),
            pltpu.VMEM((PANELS, 2, PANEL, PANEL), BF16),
            pltpu.VMEM((PANELS, 2, PANEL, PANEL), BF16),
        ],
        compiler_params=pltpu.CompilerParams(vmem_limit_bytes=48 << 20),
        name="analyse",
    )(pos, counts, priors, given, state, *planned)


def shards(
    prior_member_matrix,
    east_speed,
    north_speed,
    diffusion,
    obs_column,
    obs_comp,
    observation_reach,
    obs_owner,
    obs_order,
    obs_value,
    obs_error,
):
    comps, zonal_extent, width_y, members = prior_member_matrix.shape
    per_level = comps // east_speed.shape[0]
    here_x = lax.axis_index("gx")
    here_y = lax.axis_index("gy")
    pos = jnp.stack([here_x, here_y]).astype(jnp.int32)
    zero = jnp.zeros_like(obs_comp)
    table = jnp.stack(
        [
            obs_column[:, 0],
            obs_column[:, 1],
            obs_comp // per_level,
            observation_reach,
            obs_owner,
            obs_order,
            zero,
            zero,
        ]
    )
    perm, obs_weight, select, slots, source, place, counts = plan(pos, table)

    def rows(count, width=MEM):
        return jax.ShapeDtypeStruct((count, width), F32)

    def along_x(value, step):
        return lax.ppermute(value, "gx", [(i, (i + step) % 16) for i in range(16)])

    def along_y(value, step):
        return lax.ppermute(value, "gy", [(i, i + step) for i in range(8) if 0 <= i + step < 8])

    code = obs_column[:, 0] + obs_column[:, 1] * 256 + obs_comp * 65536
    cells = prior_member_matrix
    flat = cells.reshape(-1, members)
    speeds = [field.reshape(-1, width_y) for field in (east_speed, north_speed, diffusion)]
    own, own_coef, to_east, to_west, base_north, base_south = pl.pallas_call(
        edge_kernel,
        out_shape=(rows(104), rows(72), rows(64), rows(64), rows(48), rows(48)),
        in_specs=[smem(), smem()] + [vmem()] * 4,
        out_specs=[vmem()] * 6,
        name="edges",
    )(pos, code, flat, *speeds)
    from_west = along_x(to_east, 1)
    from_east = along_x(to_west, -1)
    to_north, to_south = pl.pallas_call(
        corner_kernel,
        out_shape=(rows(48), rows(48)),
        in_specs=[smem(), smem()] + [vmem()] * 4,
        out_specs=[vmem()] * 2,
        name="corners",
    )(pos, code, base_north, base_south, from_west, from_east)
    from_south = along_y(to_north, 1)
    from_north = along_y(to_south, -1)
    held = jnp.concatenate([obs_value.reshape(1, -1), obs_error.reshape(1, -1)], axis=1)
    held = jnp.pad(held, ((0, 0), (0, members - held.shape[1])))
    bundle = pl.pallas_call(
        prior_kernel,
        out_shape=rows(9),
        in_specs=[smem(), smem()] + [vmem()] * 7,
        out_specs=vmem(),
        scratch_shapes=[pltpu.VMEM((64, MEM), F32)],
        name="priors",
    )(pos, code, own, own_coef, from_west, from_east, from_south, from_north, held)

    bundle, late = lax.optimization_barrier((bundle, cells))
    bundle = jnp.broadcast_to(bundle.reshape(1, 9, 1, members), (128, 9, 1, members))
    arrived = lax.all_to_all(bundle, ("gx", "gy"), 0, 0, tiled=True)

    halo_w = along_x(late[:, CX - 2 :], 1)
    halo_e = along_x(late[:, :2], -1)
    wide = jnp.concatenate([halo_w[:, 1:], late, halo_e[:, :1]], axis=1)
    halo_s = along_y(wide[:, :, CY - 2 :], 1)
    halo_n = along_y(wide[:, :, :2], -1)
    state = pl.pallas_call(
        forecast_kernel,
        out_shape=jax.ShapeDtypeStruct(cells.shape, F32),
        in_specs=[vmem()] * 12,
        out_specs=vmem(),
        scratch_shapes=[
            pltpu.VMEM((4, 3, CY, 128), F32),
            pltpu.VMEM((2, CX + 4, CY + 16, MEM), F32),
            pltpu.VMEM((2, CX + 4, CY + 16, MEM), F32),
        ],
        compiler_params=pltpu.CompilerParams(vmem_limit_bytes=32 << 20),
        name="forecast",
    )(late, *speeds, halo_w, halo_e, halo_s, halo_n, from_west, from_east, from_south, from_north)
    state = state.reshape(-1, members)

    priors = arrived[:, :8].reshape(NOBS, members)
    given = arrived[:, 8].reshape(128, members)
    result = analyse(
        pos, counts, priors, given, state, perm, obs_weight, select, slots, source, place
    )
    return result.reshape(comps, zonal_extent, width_y, members)


def solution(mesh):
    return jax.shard_map(
        shards,
        mesh=mesh,
        in_specs=(
            P(None, "gx", "gy", None),
            P(None, "gx", "gy"),
            P(None, "gx", "gy"),
            P(None, "gx", "gy"),
            P(),
            P(),
            P(),
            P(),
            P(),
            P("gx", "gy", None),
            P("gx", "gy", None),
        ),
        out_specs=P(None, "gx", "gy", None),
        check_vma=False,
    )
```

```python
import jax
import jax.numpy as jnp
from jax import lax
from jax.experimental import pallas as pl
from jax.experimental.pallas import tpu as pltpu
from jax.sharding import PartitionSpec as P

FSTEPS = 2
PANEL = 256
PANELS = 4
NOBS = 1024
COMP = 8
CX = 16
CY = 32
MEM = 128
BLOCK = CX * CY
F32 = jnp.float32
BF16 = jnp.bfloat16
NT = (((1,), (1,)), ((), ()))
NN = (((1,), (0,)), ((), ()))


def dot(left, right, dims=NN):
    return lax.dot_general(left, right, dims, preferred_element_type=F32)


def halves(full):
    high = full.astype(BF16)
    low = (full - high.astype(F32)).astype(BF16)
    return high, low


def as_columns(row):
    return jnp.transpose(jnp.broadcast_to(row, (128, row.shape[1])))


def plan_kernel(pos, table, perm, obs_weight, select, slots, source, place, counts):
    here_x = pos[0]
    here_y = pos[1]
    owner = table[4:5, :]
    lane = lax.broadcasted_iota(jnp.int32, (1, NOBS), 1)
    within = lane & 7
    rank = jnp.zeros((1, NOBS), jnp.int32)
    for gap in range(1, 8):
        same = (within >= gap) & (pltpu.roll(owner, gap, 1) == owner)
        rank = rank + same.astype(jnp.int32)
    place_row = (lane >> 6) * 2 + rank
    source_row = owner * 8 + ((lane >> 3) & 7)
    facts = jnp.concatenate(
        [table[0:4, :], place_row, source_row, jnp.zeros((2, NOBS), jnp.int32)], axis=0
    ).astype(F32)
    order = as_columns(table[5:6, :].astype(F32))
    lanes = lax.broadcasted_iota(jnp.int32, (NOBS, 128), 1).astype(F32)
    for part in range(NOBS // 128):
        hit = order == lanes + float(128 * part)
        perm[:, part * 128 : (part + 1) * 128] = jnp.where(hit, 1.0, 0.0).astype(BF16)
    ordered = dot(facts.astype(BF16), perm[...], NT)

    col_x = as_columns(ordered[0:1])
    col_y = as_columns(ordered[1:2])
    col_l = as_columns(ordered[2:3])
    place[...] = as_columns(ordered[4:5])
    col_s = as_columns(ordered[5:6])
    source[...] = jnp.where(col_s == lanes, 1.0, 0.0).astype(BF16)
    inverse = 1.0 / (ordered[3:4] + 1.0)
    first = 0
    for panel in range(PANELS - 1):
        begin = (panel + 1) * PANEL
        rows = NOBS - begin
        for part in range(PANEL // 128):
            cols = slice(panel * PANEL + part * 128, panel * PANEL + (part + 1) * 128)
            gap_x = jnp.abs(col_x[begin:] - ordered[0:1, cols])
            gap_x = jnp.minimum(gap_x, 256.0 - gap_x)
            gap_y = col_y[begin:] - ordered[1:2, cols]
            near = jnp.maximum(0.0, 1.0 - (gap_x * gap_x * (1.0 / 2304.0) + gap_y * gap_y * (1.0 / 9216.0)))
            gap_l = jnp.abs(col_l[begin:] - ordered[2:3, cols])
            level = jnp.maximum(0.0, 1.0 - gap_l * inverse[:, cols])
            obs_weight[first : first + rows, part * 128 : (part + 1) * 128] = (
                near * near * level * (1.0 / (MEM - 1))
            )
        first += rows

    whole = ordered.astype(jnp.int32)
    off_x = (whole[0:1] - here_x * CX) & 255
    far_x = jnp.where(off_x < CX, 0, jnp.minimum(off_x - (CX - 1), 256 - off_x))
    off_y = whole[1:2] - here_y * CY
    far_y = jnp.maximum(0, jnp.maximum(-off_y, off_y - (CY - 1)))
    reached = jnp.where(4 * far_x * far_x + far_y * far_y < 9216, 1.0, 0.0)
    before = lax.broadcasted_iota(jnp.int32, (PANEL, PANEL), 0) < lax.broadcasted_iota(
        jnp.int32, (PANEL, PANEL), 1
    )
    before = jnp.where(before, 1.0, 0.0).astype(BF16)
    slot = lax.broadcasted_iota(jnp.int32, (PANEL, PANEL), 0).astype(F32)
    for panel in range(PANELS):
        cols = slice(panel * PANEL, (panel + 1) * PANEL)
        mask = reached[:, cols]
        ranks = dot(jnp.broadcast_to(mask, (8, PANEL)).astype(BF16), before)[0:1]
        chosen = jnp.where((slot == ranks) & (mask > 0.0), 1.0, 0.0).astype(BF16)
        select[panel] = chosen
        packed = dot(ordered[:, cols].astype(BF16), chosen, NT)
        slots[panel] = jnp.concatenate(
            [packed[0:3], 1.0 / (packed[3:4] + 1.0), packed[4:8]], axis=0
        )
        counts[panel] = jnp.sum(mask).astype(jnp.int32)


def analysis_kernel(
    pos, counts, arrived, slots, perm_far, source_far, place_far, weight_far, select_far, state_far,
    out, rows, near, left, right, perm, source, place, obs_weight, select, state, arrivals,
):
    here_x = pos[0]
    here_y = pos[1]
    copies = [
        pltpu.make_async_copy(far, close, arrivals.at[index])
        for index, (far, close) in enumerate(
            (
                (perm_far, perm),
                (source_far, source),
                (place_far, place),
                (weight_far, obs_weight),
                (select_far, select),
                (state_far, state),
            )
        )
    ]
    for copy in copies:
        copy.start()
    for k in range(8):
        rows[pl.ds(k, 128, stride=8), :] = arrived[pl.ds(k, 128, stride=9), :]
    given = arrived[pl.ds(8, 128, stride=9), :]
    high, low = halves(rows[...])
    both = jnp.concatenate([high, low], axis=1)
    copies[0].wait()
    for panel in range(PANELS):
        span = slice(panel * PANEL, (panel + 1) * PANEL)
        moved = dot(perm[span, :], both)
        rows[span, :] = moved[:, :MEM] + moved[:, MEM:]
    v_high = given.astype(BF16)
    rest = given - v_high.astype(F32)
    v_mid = rest.astype(BF16)
    v_low = (rest - v_mid.astype(F32)).astype(BF16)
    v_all = jnp.concatenate([v_high, v_mid, v_low], axis=1)
    lanes = lax.broadcasted_iota(jnp.int32, (PANEL, 128), 1).astype(F32)

    copies[1].wait()
    copies[2].wait()
    first = 0
    for panel in range(PANELS):
        span = slice(panel * PANEL, (panel + 1) * PANEL)
        held = dot(source[span, :], v_all)
        held = held[:, :128] + held[:, 128:256] + held[:, 256:]
        here = place[span, :]
        value = jnp.sum(jnp.where(lanes == here, held, 0.0), axis=1, keepdims=True)
        error = jnp.sum(jnp.where(lanes == here + 32.0, held, 0.0), axis=1, keepdims=True)
        prior = rows[span, :]
        centre = jnp.sum(prior, axis=1, keepdims=True) * (1.0 / MEM)
        spread = prior - centre
        variance = jnp.sum(spread * spread, axis=1, keepdims=True) / (MEM - 1)
        inverse = 1.0 / (variance + error)
        gain = (value - centre) * inverse
        shrink = inverse / (1.0 + jnp.sqrt(error * inverse))
        change = gain - shrink * spread
        q_high, q_low = halves(spread)
        h_high, h_low = halves(change)
        if panel < PANELS - 1:
            begin = (panel + 1) * PANEL
            count = NOBS - begin
            later = rows[begin:, :]
            l_high, l_low = halves(later - jnp.sum(later, axis=1, keepdims=True) * (1.0 / MEM))
            q_both = jnp.concatenate(
                [jnp.concatenate([q_high, q_high], axis=1), jnp.concatenate([q_low, q_low], axis=1)], axis=0
            )
            cov = dot(jnp.concatenate([l_high, l_low], axis=1), q_both, NT)
            if panel == 0:
                copies[3].wait()
            local = (cov[:, :PANEL] + cov[:, PANEL:]) * obs_weight[first : first + count, :]
            g_high, g_low = halves(local)
            h_both = jnp.concatenate([h_high, h_low], axis=1)
            step = dot(g_high, h_both) + dot(g_low, h_both)
            rows[begin:, :] = later + (step[:, :MEM] + step[:, MEM:])
            first += count
        if panel == 0:
            copies[4].wait()
        packed = dot(select[panel], jnp.concatenate([q_high, q_low, h_high, h_low], axis=1)).astype(BF16)
        for part in range(2):
            half = packed[part * 128 : (part + 1) * 128]
            q_h, q_l, h_h, h_l = (half[:, i * MEM : (i + 1) * MEM] for i in range(4))
            left[panel, part] = jnp.concatenate(
                [jnp.concatenate([q_h, q_h], axis=1), jnp.concatenate([q_l, q_l], axis=1)], axis=0
            )
            h_row = jnp.concatenate([h_h, h_l], axis=1)
            right[panel, part] = jnp.concatenate([h_row, h_row], axis=0)
        fact = slots[panel]
        step_x = lax.broadcasted_iota(jnp.int32, (CX, PANEL), 0) + here_x * CX
        gap_x = jnp.abs(step_x.astype(F32) - fact[0:1])
        gap_x = jnp.minimum(gap_x, 256.0 - gap_x)
        part_x = 1.0 - gap_x * gap_x * (1.0 / 2304.0)
        step_y = lax.broadcasted_iota(jnp.int32, (CY, PANEL), 0) + here_y * CY
        gap_y = step_y.astype(F32) - fact[1:2]
        part_y = gap_y * gap_y * (1.0 / 9216.0)
        for col in range(CX):
            close = jnp.maximum(0.0, part_x[col : col + 1] - part_y)
            near[panel, col * CY : (col + 1) * CY, :] = close * close * (1.0 / (MEM - 1))

    copies[5].wait()

    @pl.loop(0, COMP)
    def _(comp):
        level = (comp // 2).astype(F32)
        at = pl.ds(pl.multiple_of(comp * BLOCK, BLOCK), BLOCK)
        block = state[at, :]
        mean = jnp.sum(block, axis=1, keepdims=True) * (1.0 / MEM)
        out[at, :] = block - mean
        for panel in range(PANELS):
            fact = slots[panel]
            level_weight = jnp.maximum(0.0, 1.0 - jnp.abs(fact[2:3] - level) * fact[3:4])

            def local_step(both, part):
                cov = dot(both, left[panel, part], NT)
                cols = slice(part * 128, (part + 1) * 128)
                local = (cov[:, :128] + cov[:, 128:]) * (near[panel, :, cols] * level_weight[:, cols])
                g_high, g_low = halves(local)
                step = dot(jnp.concatenate([g_high, g_low], axis=1), right[panel, part])
                return step[:, :MEM] + step[:, MEM:]

            old = out[at, :]
            old_high, old_low = halves(old)
            old_both = jnp.concatenate([old_high, old_low], axis=1)
            out[at, :] = old + local_step(old_both, 0)

            @pl.when(counts[panel] > 128)
            def _():
                out[at, :] = out[at, :] + local_step(old_both, 1)
        out[at, :] = out[at, :] + mean


OFFSETS = (
    (0, 0), (-1, 0), (1, 0), (0, -1), (0, 1),
    (-1, -1), (-1, 1), (1, -1), (1, 1),
    (-2, 0), (2, 0), (0, -2), (0, 2),
)


def edge_kernel(pos, code, cells, east, north, diff, own, own_coef, to_east, to_west, to_north, to_south):
    here_x = pos[0]
    here_y = pos[1]
    coefs = (east, north, diff)

    def look(shift_x, shift_y, k):
        tile_x = (here_x + shift_x) & 15
        tile_y = jnp.clip(here_y + shift_y, 0, 7)
        word = code[(tile_x * 8 + tile_y) * 8 + k]
        return word & 15, (word >> 8) & 31, word >> 16

    def cell(comp, x, y):
        return cells[pl.ds((comp * CX + x) * CY + y, 1), :]

    def clip_x(x):
        return jnp.clip(x, 0, CX - 1)

    def clip_y(y):
        return jnp.clip(y, 0, CY - 1)

    for k in range(8):
        x, y, comp = look(0, 0, k)
        for index, (step_x, step_y) in enumerate(OFFSETS):
            at = index * 8 + k
            own[at : at + 1, :] = cell(comp, clip_x(x + step_x), clip_y(y + step_y))
        for step_x in (-1, 0, 1):
            for c in range(3):
                at = (c * 3 + step_x + 1) * 8 + k
                own_coef[at : at + 1, 0:CY] = coefs[c][pl.ds((comp >> 1) * CX + clip_x(x + step_x), 1), :]
        for shift, target, edge in ((1, to_east, CX - 1), (-1, to_west, 0)):
            x, y, comp = look(shift, 0, k)
            for index, step_y in enumerate((-1, 0, 1)):
                at = index * 8 + k
                target[at : at + 1, :] = cell(comp, edge, clip_y(y + step_y))
            target[24 + k : 25 + k, :] = cell(comp, clip_x(x + shift * (CX - 2)), y)
            _, _, comp = look(shift, 1, k)
            target[32 + k : 33 + k, :] = cell(comp, edge, CY - 1)
            _, _, comp = look(shift, -1, k)
            target[40 + k : 41 + k, :] = cell(comp, edge, 0)
        for shift, target, edge in ((1, to_north, CY - 1), (-1, to_south, 0)):
            x, y, comp = look(0, shift, k)
            for index, step_x in enumerate((-1, 0, 1)):
                at = index * 8 + k
                target[at : at + 1, :] = cell(comp, clip_x(x + step_x), edge)
            target[24 + k : 25 + k, :] = cell(comp, x, clip_y(y + shift * (CY - 2)))
    for target, edge in ((to_east, CX - 1), (to_west, 0)):
        target[48:64, :] = jnp.zeros((16, MEM), F32)
        for comp in range(COMP):
            target[64 + comp : 65 + comp, :] = cell(comp, edge, CY - 1)
            target[72 + comp : 73 + comp, :] = cell(comp, edge, 0)
        for c in range(3):
            for level in range(4):
                at = 48 + c * 4 + level
                target[at : at + 1, 0:CY] = coefs[c][level * CX + edge : level * CX + edge + 1, :]
    lanes = lax.broadcasted_iota(jnp.int32, (CX, MEM), 1)
    for target, edge in ((to_north, CY - 1), (to_south, 0)):
        table = jnp.zeros((CX, MEM), F32)
        for c in range(3):
            for level in range(4):
                line = coefs[c][level * CX : (level + 1) * CX, edge : edge + 1]
                table = jnp.where(lanes == c * 4 + level, line, table)
        target[32:48, :] = table


def obs_columns(pos, code):
    begin = (pos[0] * 8 + pos[1]) * 8
    row = lax.broadcasted_iota(jnp.int32, (8, MEM), 0)
    word = jnp.zeros((8, MEM), jnp.int32)
    for k in range(8):
        word = jnp.where(row == k, code[begin + k], word)
    return word & 15, (word >> 8) & 31, word >> 16


def corner_kernel(pos, code, base_north, base_south, from_west, from_east, to_north, to_south):
    row = lax.broadcasted_iota(jnp.int32, (8, MEM), 0)
    for shift, base, target, first in ((1, base_north, to_north, 32), (-1, base_south, to_south, 40)):
        tile_y = jnp.clip(pos[1] + shift, 0, 7)
        begin = (pos[0] * 8 + tile_y) * 8
        x = jnp.zeros((8, MEM), jnp.int32)
        for k in range(8):
            x = jnp.where(row == k, code[begin + k] & 15, x)
        target[0:48, :] = base[...]
        corners = 64 if shift == 1 else 72
        target[48:56, :] = from_west[corners : corners + 8, :]
        target[56:64, :] = from_east[corners : corners + 8, :]
        target[0:8, :] = jnp.where(x == 0, from_west[first : first + 8, :], base[0:8, :])
        target[16:24, :] = jnp.where(x == CX - 1, from_east[first : first + 8, :], base[16:24, :])


def prior_kernel(
    pos, code, own, own_coef, from_west, from_east, from_south, from_north, held, out, scratch
):
    x, y, comp = obs_columns(pos, code)
    level = comp >> 1
    west = x == 0
    east = x == CX - 1
    begin = (pos[0] * 8 + pos[1]) * 8
    for k in range(8):
        word = code[begin + k]
        here_l = word >> 17
        for c in range(3):
            at = c * 8 + k
            scratch[at : at + 1, :] = from_west[pl.ds(48 + c * 4 + here_l, 1), :]
            scratch[24 + at : 25 + at, :] = from_east[pl.ds(48 + c * 4 + here_l, 1), :]
        scratch[48 + k : 49 + k, :] = from_south[pl.ds(32 + (word & 15), 1), :]
        scratch[56 + k : 57 + k, :] = from_north[pl.ds(32 + (word & 15), 1), :]

    state = {}
    for index, (step_x, step_y) in enumerate(OFFSETS):
        value = own[index * 8 : index * 8 + 8, :]
        if step_x < 0:
            group = 3 if step_x == -2 else step_y + 1
            value = jnp.where(x + step_x < 0, from_west[group * 8 : group * 8 + 8, :], value)
        if step_x > 0:
            group = 3 if step_x == 2 else step_y + 1
            value = jnp.where(x + step_x >= CX, from_east[group * 8 : group * 8 + 8, :], value)
        if step_y < 0:
            group = 3 if step_y == -2 else step_x + 1
            value = jnp.where(y + step_y < 0, from_south[group * 8 : group * 8 + 8, :], value)
        if step_y > 0:
            group = 3 if step_y == 2 else step_x + 1
            value = jnp.where(y + step_y >= CY, from_north[group * 8 : group * 8 + 8, :], value)
        state[(step_x, step_y)] = value

    lanes = lax.broadcasted_iota(jnp.int32, (8, MEM), 1)
    at_y = lanes[:, :CY] - y[:, :CY]

    def pick(values, mask):
        return jnp.sum(jnp.where(mask, values, 0.0), axis=1, keepdims=True)

    def rows_of(c, step_x):
        at = (c * 3 + step_x + 1) * 8
        return own_coef[at : at + 8, 0:CY]

    def coefs_at(step_x, step_y):
        found = []
        for c in range(3):
            value = pick(rows_of(c, step_x), at_y == step_y)
            if step_x == -1:
                value = jnp.where(west[:, :1], pick(scratch[c * 8 : c * 8 + 8, 0:CY], at_y == 0), value)
            if step_x == 1:
                value = jnp.where(east[:, :1], pick(scratch[24 + c * 8 : 32 + c * 8, 0:CY], at_y == 0), value)
            mine = lanes == c * 4 + level
            if step_y == -1:
                value = jnp.where(y[:, :1] == 0, pick(scratch[48:56, :], mine), value)
            if step_y == 1:
                value = jnp.where(y[:, :1] == CY - 1, pick(scratch[56:64, :], mine), value)
            found.append(value)
        return found

    def advance(field, step_x, step_y):
        u, v, nu = coefs_at(step_x, step_y)
        mid = field[(step_x, step_y)]
        e = field[(step_x + 1, step_y)]
        w = field[(step_x - 1, step_y)]
        n = field[(step_x, step_y + 1)]
        s = field[(step_x, step_y - 1)]
        return mid + nu * (e + w + n + s - 4.0 * mid) - 0.5 * (u * (e - w) + v * (n - s))

    after = {key: advance(state, *key) for key in OFFSETS[:5]}
    out[0:8, :] = advance(after, 0, 0)
    out[8:9, :] = held[...]


def stencil(mid, e, w, n, s, u, v, nu):
    return mid + nu * (e + w + n + s - 4.0 * mid) - 0.5 * (u * (e - w) + v * (n - s))


def forecast_kernel(
    cells, east, north, diff, halo_w, halo_e, halo_s, halo_n, edge_w, edge_e, edge_s, edge_n,
    out, table, before, after,
):
    coefs = (east, north, diff)
    pad = jnp.zeros((128 - CX, CY), F32)
    fill = jnp.zeros((128, 128 - CY), F32)
    for c in range(3):
        for level in range(4):
            tile = coefs[c][level * CX : (level + 1) * CX, :]
            ends = jnp.concatenate(
                [
                    tile,
                    edge_w[48 + c * 4 + level : 49 + c * 4 + level, 0:CY],
                    edge_e[48 + c * 4 + level : 49 + c * 4 + level, 0:CY],
                    pad[: 128 - CX - 2],
                ],
                axis=0,
            )
            turned = jnp.transpose(jnp.concatenate([ends, fill], axis=1))
            table[level, c] = turned[0:CY, :]

    mid_rows = slice(8, 8 + CY)
    for level in range(4):
        for which in range(2):
            comp = level * 2 + which
            before[which, 2 : 2 + CX, mid_rows, :] = cells[comp]
            before[which, 0:2, mid_rows, :] = halo_w[comp]
            before[which, 2 + CX : 4 + CX, mid_rows, :] = halo_e[comp]
            for rim, edge, inner, target in ((halo_s, edge_s, 1, 7), (halo_n, edge_n, 0, 8 + CY)):
                before[which, 2 : 2 + CX, target, :] = rim[comp, :, inner, :]
                before[which, 1, target : target + 1, :] = edge[48 + comp : 49 + comp, :]
                before[which, 2 + CX, target : target + 1, :] = edge[56 + comp : 57 + comp, :]
        for col in range(-1, CX + 1):
            lane = CX if col < 0 else (CX + 1 if col == CX else col)
            u, v, nu = (
                jnp.broadcast_to(table[level, c, :, lane : lane + 1], (CY, MEM)) for c in range(3)
            )
            at = col + 2
            for which in range(2):
                after[which, at, mid_rows, :] = stencil(
                    before[which, at, mid_rows, :],
                    before[which, at + 1, mid_rows, :],
                    before[which, at - 1, mid_rows, :],
                    before[which, at, 9 : 9 + CY, :],
                    before[which, at, 7 : 7 + CY, :],
                    u, v, nu,
                )
        for rim, edge, outer, inside, target in (
            (halo_s, edge_s, 0, 0, 7),
            (halo_n, edge_n, 1, CY - 1, 8 + CY),
        ):
            u, v, nu = (
                jnp.broadcast_to(edge[32:48, c * 4 + level : c * 4 + level + 1], (CX, MEM))
                for c in range(3)
            )
            for which in range(2):
                comp = level * 2 + which
                mid = before[which, 2 : 2 + CX, target, :]
                e = before[which, 3 : 3 + CX, target, :]
                w = before[which, 1 : 1 + CX, target, :]
                far = rim[comp, :, outer, :]
                close = cells[comp, :, inside, :]
                n, s = (close, far) if target == 7 else (far, close)
                after[which, 2 : 2 + CX, target, :] = stencil(mid, e, w, n, s, u, v, nu)
        for col in range(CX):
            u, v, nu = (
                jnp.broadcast_to(table[level, c, :, col : col + 1], (CY, MEM)) for c in range(3)
            )
            at = col + 2
            for which in range(2):
                out[level * 2 + which, col] = stencil(
                    after[which, at, mid_rows, :],
                    after[which, at + 1, mid_rows, :],
                    after[which, at - 1, mid_rows, :],
                    after[which, at, 9 : 9 + CY, :],
                    after[which, at, 7 : 7 + CY, :],
                    u, v, nu,
                )


def vmem():
    return pl.BlockSpec(memory_space=pltpu.VMEM)


def smem():
    return pl.BlockSpec(memory_space=pltpu.SMEM)


def plan(pos, table):
    shapes = (
        jax.ShapeDtypeStruct((NOBS, NOBS), BF16),
        jax.ShapeDtypeStruct((6 * PANEL, PANEL), F32),
        jax.ShapeDtypeStruct((PANELS, PANEL, PANEL), BF16),
        jax.ShapeDtypeStruct((PANELS, 8, PANEL), F32),
        jax.ShapeDtypeStruct((NOBS, 128), BF16),
        jax.ShapeDtypeStruct((NOBS, 128), F32),
        jax.ShapeDtypeStruct((PANELS,), jnp.int32),
    )
    return pl.pallas_call(
        plan_kernel,
        out_shape=shapes,
        in_specs=[smem(), vmem()],
        out_specs=[vmem()] * 6 + [smem()],
        name="plan",
    )(pos, table)


def analyse(pos, counts, arrived, slots, *far):
    return pl.pallas_call(
        analysis_kernel,
        out_shape=jax.ShapeDtypeStruct(far[-1].shape, F32),
        in_specs=[smem(), smem(), vmem(), vmem()] + [pl.BlockSpec(memory_space=pl.ANY)] * len(far),
        out_specs=vmem(),
        scratch_shapes=[
            pltpu.VMEM((NOBS, MEM), F32),
            pltpu.VMEM((PANELS, BLOCK, PANEL), F32),
            pltpu.VMEM((PANELS, 2, PANEL, PANEL), BF16),
            pltpu.VMEM((PANELS, 2, PANEL, PANEL), BF16),
        ]
        + [pltpu.VMEM(array.shape, array.dtype) for array in far]
        + [pltpu.SemaphoreType.DMA((len(far),))],
        compiler_params=pltpu.CompilerParams(vmem_limit_bytes=40 << 20),
        name="analyse",
    )(pos, counts, arrived, slots, *far)


def shards(
    prior_member_matrix,
    east_speed,
    north_speed,
    diffusion,
    obs_column,
    obs_comp,
    observation_reach,
    obs_owner,
    obs_order,
    obs_value,
    obs_error,
):
    comps, zonal_extent, width_y, members = prior_member_matrix.shape
    per_level = comps // east_speed.shape[0]
    here_x = lax.axis_index("gx")
    here_y = lax.axis_index("gy")
    pos = jnp.stack([here_x, here_y]).astype(jnp.int32)
    zero = jnp.zeros_like(obs_comp)
    table = jnp.stack(
        [
            obs_column[:, 0],
            obs_column[:, 1],
            obs_comp // per_level,
            observation_reach,
            obs_owner,
            obs_order,
            zero,
            zero,
        ]
    )
    perm, obs_weight, select, slots, source, place, counts = plan(pos, table)

    def rows(count, width=MEM):
        return jax.ShapeDtypeStruct((count, width), F32)

    def along_x(value, step):
        return lax.ppermute(value, "gx", [(i, (i + step) % 16) for i in range(16)])

    def along_y(value, step):
        return lax.ppermute(value, "gy", [(i, i + step) for i in range(8) if 0 <= i + step < 8])

    code = obs_column[:, 0] + obs_column[:, 1] * 256 + obs_comp * 65536
    cells = prior_member_matrix
    flat = cells.reshape(-1, members)
    speeds = [field.reshape(-1, width_y) for field in (east_speed, north_speed, diffusion)]
    own, own_coef, to_east, to_west, base_north, base_south = pl.pallas_call(
        edge_kernel,
        out_shape=(rows(104), rows(72), rows(80), rows(80), rows(48), rows(48)),
        in_specs=[smem(), smem()] + [vmem()] * 4,
        out_specs=[vmem()] * 6,
        name="edges",
    )(pos, code, flat, *speeds)
    from_west = along_x(to_east, 1)
    from_east = along_x(to_west, -1)
    from_west, from_east, late = lax.optimization_barrier((from_west, from_east, cells))
    halo_w = along_x(late[:, CX - 2 :], 1)
    halo_e = along_x(late[:, :2], -1)
    halo_s = along_y(late[:, :, CY - 2 :], 1)
    halo_n = along_y(late[:, :, :2], -1)
    to_north, to_south = pl.pallas_call(
        corner_kernel,
        out_shape=(rows(64), rows(64)),
        in_specs=[smem(), smem()] + [vmem()] * 4,
        out_specs=[vmem()] * 2,
        name="corners",
    )(pos, code, base_north, base_south, from_west, from_east)
    from_south = along_y(to_north, 1)
    from_north = along_y(to_south, -1)
    held = jnp.concatenate([obs_value.reshape(1, -1), obs_error.reshape(1, -1)], axis=1)
    held = jnp.pad(held, ((0, 0), (0, members - held.shape[1])))
    bundle = pl.pallas_call(
        prior_kernel,
        out_shape=rows(9),
        in_specs=[smem(), smem()] + [vmem()] * 7,
        out_specs=vmem(),
        scratch_shapes=[pltpu.VMEM((64, MEM), F32)],
        name="priors",
    )(pos, code, own, own_coef, from_west, from_east, from_south, from_north, held)

    bundle = jnp.broadcast_to(bundle.reshape(1, 9, 1, members), (128, 9, 1, members))
    arrived = lax.all_to_all(bundle, ("gx", "gy"), 0, 0, tiled=True)

    state = pl.pallas_call(
        forecast_kernel,
        out_shape=jax.ShapeDtypeStruct(cells.shape, F32),
        in_specs=[vmem()] * 12,
        out_specs=vmem(),
        scratch_shapes=[
            pltpu.VMEM((4, 3, CY, 128), F32),
            pltpu.VMEM((2, CX + 4, CY + 16, MEM), F32),
            pltpu.VMEM((2, CX + 4, CY + 16, MEM), F32),
        ],
        compiler_params=pltpu.CompilerParams(vmem_limit_bytes=32 << 20),
        name="forecast",
    )(cells, *speeds, halo_w, halo_e, halo_s, halo_n, from_west, from_east, from_south, from_north)
    state = state.reshape(-1, members)

    result = analyse(
        pos, counts, arrived.reshape(-1, members), slots, perm, source, place, obs_weight, select, state
    )
    return result.reshape(comps, zonal_extent, width_y, members)


def solution(mesh):
    return jax.shard_map(
        shards,
        mesh=mesh,
        in_specs=(
            P(None, "gx", "gy", None),
            P(None, "gx", "gy"),
            P(None, "gx", "gy"),
            P(None, "gx", "gy"),
            P(),
            P(),
            P(),
            P(),
            P(),
            P("gx", "gy", None),
            P("gx", "gy", None),
        ),
        out_specs=P(None, "gx", "gy", None),
        check_vma=False,
    )
```

```python
import jax
import jax.numpy as jnp
from jax import lax
from jax.experimental import pallas as pl
from jax.experimental.pallas import tpu as pltpu
from jax.sharding import PartitionSpec as P

FSTEPS = 2
PANEL = 256
PANELS = 4
NOBS = 1024
COMP = 8
CX = 16
CY = 32
MEM = 128
BLOCK = CX * CY
F32 = jnp.float32
BF16 = jnp.bfloat16
NT = (((1,), (1,)), ((), ()))
NN = (((1,), (0,)), ((), ()))


def dot(left, right, dims=NN):
    return lax.dot_general(left, right, dims, preferred_element_type=F32)


def halves(full):
    high = full.astype(BF16)
    low = (full - high.astype(F32)).astype(BF16)
    return high, low


def as_columns(row):
    return jnp.transpose(jnp.broadcast_to(row, (128, row.shape[1])))


def plan_kernel(pos, table, perm, obs_weight, select, slots, source, place, counts):
    here_x = pos[0]
    here_y = pos[1]
    owner = table[4:5, :]
    lane = lax.broadcasted_iota(jnp.int32, (1, NOBS), 1)
    within = lane & 7
    rank = jnp.zeros((1, NOBS), jnp.int32)
    for gap in range(1, 8):
        same = (within >= gap) & (pltpu.roll(owner, gap, 1) == owner)
        rank = rank + same.astype(jnp.int32)
    place_row = (lane >> 6) * 2 + rank
    source_row = owner * 8 + ((lane >> 3) & 7)
    facts = jnp.concatenate(
        [table[0:4, :], place_row, source_row, jnp.zeros((2, NOBS), jnp.int32)], axis=0
    ).astype(F32)
    order = as_columns(table[5:6, :].astype(F32))
    lanes = lax.broadcasted_iota(jnp.int32, (NOBS, 128), 1).astype(F32)
    for part in range(NOBS // 128):
        hit = order == lanes + float(128 * part)
        perm[:, part * 128 : (part + 1) * 128] = jnp.where(hit, 1.0, 0.0).astype(BF16)
    ordered = dot(facts.astype(BF16), perm[...], NT)

    col_x = as_columns(ordered[0:1])
    col_y = as_columns(ordered[1:2])
    col_l = as_columns(ordered[2:3])
    place[...] = as_columns(ordered[4:5])
    col_s = as_columns(ordered[5:6])
    source[...] = jnp.where(col_s == lanes, 1.0, 0.0).astype(BF16)
    inverse = 1.0 / (ordered[3:4] + 1.0)
    first = 0
    for panel in range(PANELS - 1):
        begin = (panel + 1) * PANEL
        rows = NOBS - begin
        for part in range(PANEL // 128):
            cols = slice(panel * PANEL + part * 128, panel * PANEL + (part + 1) * 128)
            gap_x = jnp.abs(col_x[begin:] - ordered[0:1, cols])
            gap_x = jnp.minimum(gap_x, 256.0 - gap_x)
            gap_y = col_y[begin:] - ordered[1:2, cols]
            near = jnp.maximum(0.0, 1.0 - (gap_x * gap_x * (1.0 / 2304.0) + gap_y * gap_y * (1.0 / 9216.0)))
            gap_l = jnp.abs(col_l[begin:] - ordered[2:3, cols])
            level = jnp.maximum(0.0, 1.0 - gap_l * inverse[:, cols])
            obs_weight[first : first + rows, part * 128 : (part + 1) * 128] = (
                near * near * level * (1.0 / (MEM - 1))
            )
        first += rows

    whole = ordered.astype(jnp.int32)
    off_x = (whole[0:1] - here_x * CX) & 255
    far_x = jnp.where(off_x < CX, 0, jnp.minimum(off_x - (CX - 1), 256 - off_x))
    off_y = whole[1:2] - here_y * CY
    far_y = jnp.maximum(0, jnp.maximum(-off_y, off_y - (CY - 1)))
    reached = jnp.where(4 * far_x * far_x + far_y * far_y < 9216, 1.0, 0.0)
    before = lax.broadcasted_iota(jnp.int32, (PANEL, PANEL), 0) < lax.broadcasted_iota(
        jnp.int32, (PANEL, PANEL), 1
    )
    before = jnp.where(before, 1.0, 0.0).astype(BF16)
    slot = lax.broadcasted_iota(jnp.int32, (PANEL, PANEL), 0).astype(F32)
    for panel in range(PANELS):
        cols = slice(panel * PANEL, (panel + 1) * PANEL)
        mask = reached[:, cols]
        ranks = dot(jnp.broadcast_to(mask, (8, PANEL)).astype(BF16), before)[0:1]
        chosen = jnp.where((slot == ranks) & (mask > 0.0), 1.0, 0.0).astype(BF16)
        select[panel] = chosen
        packed = dot(ordered[:, cols].astype(BF16), chosen, NT)
        slots[panel] = jnp.concatenate(
            [packed[0:3], 1.0 / (packed[3:4] + 1.0), packed[4:8]], axis=0
        )
        counts[panel] = jnp.sum(mask).astype(jnp.int32)


def analysis_kernel(
    pos, counts, arrived, slots, perm_far, source_far, place_far, weight_far, select_far, state_far,
    out, rows, near, left, right, perm, source, place, obs_weight, select, state, arrivals,
):
    here_x = pos[0]
    here_y = pos[1]
    copies = [
        pltpu.make_async_copy(far, close, arrivals.at[index])
        for index, (far, close) in enumerate(
            (
                (perm_far, perm),
                (source_far, source),
                (place_far, place),
                (weight_far, obs_weight),
                (select_far, select),
                (state_far, state),
            )
        )
    ]
    for copy in copies:
        copy.start()
    for k in range(8):
        rows[pl.ds(k, 128, stride=8), :] = arrived[pl.ds(k, 128, stride=9), :]
    given = arrived[pl.ds(8, 128, stride=9), :]
    high, low = halves(rows[...])
    both = jnp.concatenate([high, low], axis=1)
    copies[0].wait()
    for panel in range(PANELS):
        span = slice(panel * PANEL, (panel + 1) * PANEL)
        moved = dot(perm[span, :], both)
        rows[span, :] = moved[:, :MEM] + moved[:, MEM:]
    v_high = given.astype(BF16)
    rest = given - v_high.astype(F32)
    v_mid = rest.astype(BF16)
    v_low = (rest - v_mid.astype(F32)).astype(BF16)
    v_all = jnp.concatenate([v_high, v_mid, v_low], axis=1)
    lanes = lax.broadcasted_iota(jnp.int32, (PANEL, 128), 1).astype(F32)

    copies[1].wait()
    copies[2].wait()
    first = 0
    for panel in range(PANELS):
        span = slice(panel * PANEL, (panel + 1) * PANEL)
        held = dot(source[span, :], v_all)
        held = held[:, :128] + held[:, 128:256] + held[:, 256:]
        here = place[span, :]
        value = jnp.sum(jnp.where(lanes == here, held, 0.0), axis=1, keepdims=True)
        error = jnp.sum(jnp.where(lanes == here + 32.0, held, 0.0), axis=1, keepdims=True)
        prior = rows[span, :]
        centre = jnp.sum(prior, axis=1, keepdims=True) * (1.0 / MEM)
        spread = prior - centre
        variance = jnp.sum(spread * spread, axis=1, keepdims=True) / (MEM - 1)
        inverse = 1.0 / (variance + error)
        gain = (value - centre) * inverse
        shrink = inverse / (1.0 + jnp.sqrt(error * inverse))
        change = gain - shrink * spread
        q_high, q_low = halves(spread)
        h_high, h_low = halves(change)
        if panel < PANELS - 1:
            begin = (panel + 1) * PANEL
            count = NOBS - begin
            later = rows[begin:, :]
            l_high, l_low = halves(later - jnp.sum(later, axis=1, keepdims=True) * (1.0 / MEM))
            q_both = jnp.concatenate(
                [jnp.concatenate([q_high, q_high], axis=1), jnp.concatenate([q_low, q_low], axis=1)], axis=0
            )
            cov = dot(jnp.concatenate([l_high, l_low], axis=1), q_both, NT)
            if panel == 0:
                copies[3].wait()
            local = (cov[:, :PANEL] + cov[:, PANEL:]) * obs_weight[first : first + count, :]
            g_high, g_low = halves(local)
            h_both = jnp.concatenate([h_high, h_low], axis=1)
            step = dot(g_high, h_both) + dot(g_low, h_both)
            rows[begin:, :] = later + (step[:, :MEM] + step[:, MEM:])
            first += count
        if panel == 0:
            copies[4].wait()
        packed = dot(select[panel], jnp.concatenate([q_high, q_low, h_high, h_low], axis=1)).astype(BF16)
        for part in range(2):
            half = packed[part * 128 : (part + 1) * 128]
            q_h, q_l, h_h, h_l = (half[:, i * MEM : (i + 1) * MEM] for i in range(4))
            left[panel, part] = jnp.concatenate(
                [jnp.concatenate([q_h, q_h], axis=1), jnp.concatenate([q_l, q_l], axis=1)], axis=0
            )
            h_row = jnp.concatenate([h_h, h_l], axis=1)
            right[panel, part] = jnp.concatenate([h_row, h_row], axis=0)
        fact = slots[panel]
        step_x = lax.broadcasted_iota(jnp.int32, (CX, PANEL), 0) + here_x * CX
        gap_x = jnp.abs(step_x.astype(F32) - fact[0:1])
        gap_x = jnp.minimum(gap_x, 256.0 - gap_x)
        part_x = 1.0 - gap_x * gap_x * (1.0 / 2304.0)
        step_y = lax.broadcasted_iota(jnp.int32, (CY, PANEL), 0) + here_y * CY
        gap_y = step_y.astype(F32) - fact[1:2]
        part_y = gap_y * gap_y * (1.0 / 9216.0)
        for col in range(CX):
            close = jnp.maximum(0.0, part_x[col : col + 1] - part_y)
            near[panel, col * CY : (col + 1) * CY, :] = close * close * (1.0 / (MEM - 1))

    copies[5].wait()

    @pl.loop(0, COMP)
    def _(comp):
        level = (comp // 2).astype(F32)
        at = pl.ds(pl.multiple_of(comp * BLOCK, BLOCK), BLOCK)
        block = state[at, :]
        mean = jnp.sum(block, axis=1, keepdims=True) * (1.0 / MEM)
        out[at, :] = block - mean
        for panel in range(PANELS):
            fact = slots[panel]
            level_weight = jnp.maximum(0.0, 1.0 - jnp.abs(fact[2:3] - level) * fact[3:4])

            def local_step(both, part):
                cov = dot(both, left[panel, part], NT)
                cols = slice(part * 128, (part + 1) * 128)
                local = (cov[:, :128] + cov[:, 128:]) * (near[panel, :, cols] * level_weight[:, cols])
                g_high, g_low = halves(local)
                step = dot(jnp.concatenate([g_high, g_low], axis=1), right[panel, part])
                return step[:, :MEM] + step[:, MEM:]

            old = out[at, :]
            old_high, old_low = halves(old)
            old_both = jnp.concatenate([old_high, old_low], axis=1)
            out[at, :] = old + local_step(old_both, 0)

            @pl.when(counts[panel] > 128)
            def _():
                out[at, :] = out[at, :] + local_step(old_both, 1)
        out[at, :] = out[at, :] + mean


OFFSETS = (
    (0, 0), (-1, 0), (1, 0), (0, -1), (0, 1),
    (-1, -1), (-1, 1), (1, -1), (1, 1),
    (-2, 0), (2, 0), (0, -2), (0, 2),
)


def edge_kernel(pos, code, cells, east, north, diff, own, own_coef, to_east, to_west, to_north, to_south):
    here_x = pos[0]
    here_y = pos[1]
    coefs = (east, north, diff)

    def look(shift_x, shift_y, k):
        tile_x = (here_x + shift_x) & 15
        tile_y = jnp.clip(here_y + shift_y, 0, 7)
        word = code[(tile_x * 8 + tile_y) * 8 + k]
        return word & 15, (word >> 8) & 31, word >> 16

    def cell(comp, x, y):
        return cells[pl.ds((comp * CX + x) * CY + y, 1), :]

    def clip_x(x):
        return jnp.clip(x, 0, CX - 1)

    def clip_y(y):
        return jnp.clip(y, 0, CY - 1)

    for k in range(8):
        x, y, comp = look(0, 0, k)
        for index, (step_x, step_y) in enumerate(OFFSETS):
            at = index * 8 + k
            own[at : at + 1, :] = cell(comp, clip_x(x + step_x), clip_y(y + step_y))
        for step_x in (-1, 0, 1):
            for c in range(3):
                at = (c * 3 + step_x + 1) * 8 + k
                own_coef[at : at + 1, 0:CY] = coefs[c][pl.ds((comp >> 1) * CX + clip_x(x + step_x), 1), :]
        for shift, target, edge in ((1, to_east, CX - 1), (-1, to_west, 0)):
            x, y, comp = look(shift, 0, k)
            for index, step_y in enumerate((-1, 0, 1)):
                at = index * 8 + k
                target[at : at + 1, :] = cell(comp, edge, clip_y(y + step_y))
            target[24 + k : 25 + k, :] = cell(comp, clip_x(x + shift * (CX - 2)), y)
            _, _, comp = look(shift, 1, k)
            target[32 + k : 33 + k, :] = cell(comp, edge, CY - 1)
            _, _, comp = look(shift, -1, k)
            target[40 + k : 41 + k, :] = cell(comp, edge, 0)
        for shift, target, edge in ((1, to_north, CY - 1), (-1, to_south, 0)):
            x, y, comp = look(0, shift, k)
            for index, step_x in enumerate((-1, 0, 1)):
                at = index * 8 + k
                target[at : at + 1, :] = cell(comp, clip_x(x + step_x), edge)
            target[24 + k : 25 + k, :] = cell(comp, x, clip_y(y + shift * (CY - 2)))
    for target, edge in ((to_east, CX - 1), (to_west, 0)):
        target[48:64, :] = jnp.zeros((16, MEM), F32)
        for comp in range(COMP):
            target[64 + comp : 65 + comp, :] = cell(comp, edge, CY - 1)
            target[72 + comp : 73 + comp, :] = cell(comp, edge, 0)
        for c in range(3):
            for level in range(4):
                at = 48 + c * 4 + level
                target[at : at + 1, 0:CY] = coefs[c][level * CX + edge : level * CX + edge + 1, :]
    lanes = lax.broadcasted_iota(jnp.int32, (CX, MEM), 1)
    for target, edge in ((to_north, CY - 1), (to_south, 0)):
        table = jnp.zeros((CX, MEM), F32)
        for c in range(3):
            for level in range(4):
                line = coefs[c][level * CX : (level + 1) * CX, edge : edge + 1]
                table = jnp.where(lanes == c * 4 + level, line, table)
        target[32:48, :] = table


def obs_columns(pos, code):
    begin = (pos[0] * 8 + pos[1]) * 8
    row = lax.broadcasted_iota(jnp.int32, (8, MEM), 0)
    word = jnp.zeros((8, MEM), jnp.int32)
    for k in range(8):
        word = jnp.where(row == k, code[begin + k], word)
    return word & 15, (word >> 8) & 31, word >> 16


def corner_kernel(pos, code, base_north, base_south, from_west, from_east, to_north, to_south):
    row = lax.broadcasted_iota(jnp.int32, (8, MEM), 0)
    for shift, base, target, first in ((1, base_north, to_north, 32), (-1, base_south, to_south, 40)):
        tile_y = jnp.clip(pos[1] + shift, 0, 7)
        begin = (pos[0] * 8 + tile_y) * 8
        x = jnp.zeros((8, MEM), jnp.int32)
        for k in range(8):
            x = jnp.where(row == k, code[begin + k] & 15, x)
        target[0:48, :] = base[...]
        corners = 64 if shift == 1 else 72
        target[48:56, :] = from_west[corners : corners + 8, :]
        target[56:64, :] = from_east[corners : corners + 8, :]
        target[0:8, :] = jnp.where(x == 0, from_west[first : first + 8, :], base[0:8, :])
        target[16:24, :] = jnp.where(x == CX - 1, from_east[first : first + 8, :], base[16:24, :])


def prior_kernel(
    pos, code, own, own_coef, from_west, from_east, from_south, from_north, held, out, scratch
):
    x, y, comp = obs_columns(pos, code)
    level = comp >> 1
    west = x == 0
    east = x == CX - 1
    begin = (pos[0] * 8 + pos[1]) * 8
    for k in range(8):
        word = code[begin + k]
        here_l = word >> 17
        for c in range(3):
            at = c * 8 + k
            scratch[at : at + 1, :] = from_west[pl.ds(48 + c * 4 + here_l, 1), :]
            scratch[24 + at : 25 + at, :] = from_east[pl.ds(48 + c * 4 + here_l, 1), :]
        scratch[48 + k : 49 + k, :] = from_south[pl.ds(32 + (word & 15), 1), :]
        scratch[56 + k : 57 + k, :] = from_north[pl.ds(32 + (word & 15), 1), :]

    state = {}
    for index, (step_x, step_y) in enumerate(OFFSETS):
        value = own[index * 8 : index * 8 + 8, :]
        if step_x < 0:
            group = 3 if step_x == -2 else step_y + 1
            value = jnp.where(x + step_x < 0, from_west[group * 8 : group * 8 + 8, :], value)
        if step_x > 0:
            group = 3 if step_x == 2 else step_y + 1
            value = jnp.where(x + step_x >= CX, from_east[group * 8 : group * 8 + 8, :], value)
        if step_y < 0:
            group = 3 if step_y == -2 else step_x + 1
            value = jnp.where(y + step_y < 0, from_south[group * 8 : group * 8 + 8, :], value)
        if step_y > 0:
            group = 3 if step_y == 2 else step_x + 1
            value = jnp.where(y + step_y >= CY, from_north[group * 8 : group * 8 + 8, :], value)
        state[(step_x, step_y)] = value

    lanes = lax.broadcasted_iota(jnp.int32, (8, MEM), 1)
    at_y = lanes[:, :CY] - y[:, :CY]

    def pick(values, mask):
        return jnp.sum(jnp.where(mask, values, 0.0), axis=1, keepdims=True)

    def rows_of(c, step_x):
        at = (c * 3 + step_x + 1) * 8
        return own_coef[at : at + 8, 0:CY]

    def coefs_at(step_x, step_y):
        found = []
        for c in range(3):
            value = pick(rows_of(c, step_x), at_y == step_y)
            if step_x == -1:
                value = jnp.where(west[:, :1], pick(scratch[c * 8 : c * 8 + 8, 0:CY], at_y == 0), value)
            if step_x == 1:
                value = jnp.where(east[:, :1], pick(scratch[24 + c * 8 : 32 + c * 8, 0:CY], at_y == 0), value)
            mine = lanes == c * 4 + level
            if step_y == -1:
                value = jnp.where(y[:, :1] == 0, pick(scratch[48:56, :], mine), value)
            if step_y == 1:
                value = jnp.where(y[:, :1] == CY - 1, pick(scratch[56:64, :], mine), value)
            found.append(value)
        return found

    def advance(field, step_x, step_y):
        u, v, nu = coefs_at(step_x, step_y)
        mid = field[(step_x, step_y)]
        e = field[(step_x + 1, step_y)]
        w = field[(step_x - 1, step_y)]
        n = field[(step_x, step_y + 1)]
        s = field[(step_x, step_y - 1)]
        return mid + nu * (e + w + n + s - 4.0 * mid) - 0.5 * (u * (e - w) + v * (n - s))

    after = {key: advance(state, *key) for key in OFFSETS[:5]}
    out[0:8, :] = advance(after, 0, 0)
    out[8:9, :] = held[...]


def stencil(mid, e, w, n, s, u, v, nu):
    return mid + nu * (e + w + n + s - 4.0 * mid) - 0.5 * (u * (e - w) + v * (n - s))


def forecast_kernel(
    cells, east, north, diff, halo_w, halo_e, halo_s, halo_n, edge_w, edge_e, edge_s, edge_n,
    out, table, before, after, arrivals,
):
    rows = pl.ds(8, CY)
    copies = []
    for level in range(4):
        pair = pl.ds(level * 2, 2)
        copies.append(
            [
                pltpu.make_async_copy(far.at[pair], before.at[pair, cols, rows, :], arrivals.at[level])
                for far, cols in ((cells, pl.ds(2, CX)), (halo_w, pl.ds(0, 2)), (halo_e, pl.ds(2 + CX, 2)))
            ]
        )
        for copy in copies[level]:
            copy.start()
    coefs = (east, north, diff)
    pad = jnp.zeros((128 - CX, CY), F32)
    fill = jnp.zeros((128, 128 - CY), F32)
    for c in range(3):
        for level in range(4):
            tile = coefs[c][level * CX : (level + 1) * CX, :]
            ends = jnp.concatenate(
                [
                    tile,
                    edge_w[48 + c * 4 + level : 49 + c * 4 + level, 0:CY],
                    edge_e[48 + c * 4 + level : 49 + c * 4 + level, 0:CY],
                    pad[: 128 - CX - 2],
                ],
                axis=0,
            )
            turned = jnp.transpose(jnp.concatenate([ends, fill], axis=1))
            table[level, c] = turned[0:CY, :]

    mid_rows = slice(8, 8 + CY)
    for level in range(4):
        for copy in copies[level]:
            copy.wait()
        for which in range(2):
            comp = level * 2 + which
            for rim, edge, inner, target in ((halo_s, edge_s, 1, 7), (halo_n, edge_n, 0, 8 + CY)):
                before[level * 2 + which, 2 : 2 + CX, target, :] = rim[comp, :, inner, :]
                before[level * 2 + which, 1, target : target + 1, :] = edge[48 + comp : 49 + comp, :]
                before[level * 2 + which, 2 + CX, target : target + 1, :] = edge[56 + comp : 57 + comp, :]
        for col in range(-1, CX + 1):
            lane = CX if col < 0 else (CX + 1 if col == CX else col)
            u, v, nu = (
                jnp.broadcast_to(table[level, c, :, lane : lane + 1], (CY, MEM)) for c in range(3)
            )
            at = col + 2
            for which in range(2):
                after[which, at, mid_rows, :] = stencil(
                    before[level * 2 + which, at, mid_rows, :],
                    before[level * 2 + which, at + 1, mid_rows, :],
                    before[level * 2 + which, at - 1, mid_rows, :],
                    before[level * 2 + which, at, 9 : 9 + CY, :],
                    before[level * 2 + which, at, 7 : 7 + CY, :],
                    u, v, nu,
                )
        for rim, edge, outer, inside, target in (
            (halo_s, edge_s, 0, 0, 7),
            (halo_n, edge_n, 1, CY - 1, 8 + CY),
        ):
            u, v, nu = (
                jnp.broadcast_to(edge[32:48, c * 4 + level : c * 4 + level + 1], (CX, MEM))
                for c in range(3)
            )
            for which in range(2):
                comp = level * 2 + which
                mid = before[level * 2 + which, 2 : 2 + CX, target, :]
                e = before[level * 2 + which, 3 : 3 + CX, target, :]
                w = before[level * 2 + which, 1 : 1 + CX, target, :]
                far = rim[comp, :, outer, :]
                close = before[comp, 2 : 2 + CX, 8 + inside, :]
                n, s = (close, far) if target == 7 else (far, close)
                after[which, 2 : 2 + CX, target, :] = stencil(mid, e, w, n, s, u, v, nu)
        for col in range(CX):
            u, v, nu = (
                jnp.broadcast_to(table[level, c, :, col : col + 1], (CY, MEM)) for c in range(3)
            )
            at = col + 2
            for which in range(2):
                out[level * 2 + which, col] = stencil(
                    after[which, at, mid_rows, :],
                    after[which, at + 1, mid_rows, :],
                    after[which, at - 1, mid_rows, :],
                    after[which, at, 9 : 9 + CY, :],
                    after[which, at, 7 : 7 + CY, :],
                    u, v, nu,
                )


def vmem():
    return pl.BlockSpec(memory_space=pltpu.VMEM)


def hbm():
    return pl.BlockSpec(memory_space=pltpu.HBM)


def smem():
    return pl.BlockSpec(memory_space=pltpu.SMEM)


def plan(pos, table):
    shapes = (
        jax.ShapeDtypeStruct((NOBS, NOBS), BF16),
        jax.ShapeDtypeStruct((6 * PANEL, PANEL), F32),
        jax.ShapeDtypeStruct((PANELS, PANEL, PANEL), BF16),
        jax.ShapeDtypeStruct((PANELS, 8, PANEL), F32),
        jax.ShapeDtypeStruct((NOBS, 128), BF16),
        jax.ShapeDtypeStruct((NOBS, 128), F32),
        jax.ShapeDtypeStruct((PANELS,), jnp.int32),
    )
    return pl.pallas_call(
        plan_kernel,
        out_shape=shapes,
        in_specs=[smem(), vmem()],
        out_specs=[vmem()] * 6 + [smem()],
        name="plan",
    )(pos, table)


def analyse(pos, counts, arrived, slots, *far):
    return pl.pallas_call(
        analysis_kernel,
        out_shape=jax.ShapeDtypeStruct(far[-1].shape, F32),
        in_specs=[smem(), smem(), vmem(), vmem()] + [hbm()] * len(far),
        out_specs=vmem(),
        scratch_shapes=[
            pltpu.VMEM((NOBS, MEM), F32),
            pltpu.VMEM((PANELS, BLOCK, PANEL), F32),
            pltpu.VMEM((PANELS, 2, PANEL, PANEL), BF16),
            pltpu.VMEM((PANELS, 2, PANEL, PANEL), BF16),
        ]
        + [pltpu.VMEM(array.shape, array.dtype) for array in far]
        + [pltpu.SemaphoreType.DMA((len(far),))],
        compiler_params=pltpu.CompilerParams(vmem_limit_bytes=40 << 20),
        name="analyse",
    )(pos, counts, arrived, slots, *far)


def shards(
    prior_member_matrix,
    east_speed,
    north_speed,
    diffusion,
    obs_column,
    obs_comp,
    observation_reach,
    obs_owner,
    obs_order,
    obs_value,
    obs_error,
):
    comps, zonal_extent, width_y, members = prior_member_matrix.shape
    per_level = comps // east_speed.shape[0]
    here_x = lax.axis_index("gx")
    here_y = lax.axis_index("gy")
    pos = jnp.stack([here_x, here_y]).astype(jnp.int32)
    zero = jnp.zeros_like(obs_comp)
    table = jnp.stack(
        [
            obs_column[:, 0],
            obs_column[:, 1],
            obs_comp // per_level,
            observation_reach,
            obs_owner,
            obs_order,
            zero,
            zero,
        ]
    )

    def rows(count, width=MEM):
        return jax.ShapeDtypeStruct((count, width), F32)

    def along_x(value, step):
        return lax.ppermute(value, "gx", [(i, (i + step) % 16) for i in range(16)])

    def along_y(value, step):
        return lax.ppermute(value, "gy", [(i, i + step) for i in range(8) if 0 <= i + step < 8])

    code = obs_column[:, 0] + obs_column[:, 1] * 256 + obs_comp * 65536
    cells = prior_member_matrix
    flat = cells.reshape(-1, members)
    speeds = [field.reshape(-1, width_y) for field in (east_speed, north_speed, diffusion)]
    own, own_coef, to_east, to_west, base_north, base_south = pl.pallas_call(
        edge_kernel,
        out_shape=(rows(104), rows(72), rows(80), rows(80), rows(48), rows(48)),
        in_specs=[smem(), smem()] + [vmem()] * 4,
        out_specs=[vmem()] * 6,
        name="edges",
    )(pos, code, flat, *speeds)
    from_west = along_x(to_east, 1)
    from_east = along_x(to_west, -1)
    from_west, from_east, late = lax.optimization_barrier((from_west, from_east, cells))
    halo_w = along_x(late[:, CX - 2 :], 1)
    halo_e = along_x(late[:, :2], -1)
    halo_s = along_y(late[:, :, CY - 2 :], 1)
    halo_n = along_y(late[:, :, :2], -1)
    to_north, to_south = pl.pallas_call(
        corner_kernel,
        out_shape=(rows(64), rows(64)),
        in_specs=[smem(), smem()] + [vmem()] * 4,
        out_specs=[vmem()] * 2,
        name="corners",
    )(pos, code, base_north, base_south, from_west, from_east)
    from_south = along_y(to_north, 1)
    from_north = along_y(to_south, -1)
    held = jnp.concatenate([obs_value.reshape(1, -1), obs_error.reshape(1, -1)], axis=1)
    held = jnp.pad(held, ((0, 0), (0, members - held.shape[1])))
    bundle = pl.pallas_call(
        prior_kernel,
        out_shape=rows(9),
        in_specs=[smem(), smem()] + [vmem()] * 7,
        out_specs=vmem(),
        scratch_shapes=[pltpu.VMEM((64, MEM), F32)],
        name="priors",
    )(pos, code, own, own_coef, from_west, from_east, from_south, from_north, held)

    bundle, table, halo_w, halo_e, halo_s, halo_n = lax.optimization_barrier(
        (bundle, table, halo_w, halo_e, halo_s, halo_n)
    )
    perm, obs_weight, select, slots, source, place, counts = plan(pos, table)
    bundle = jnp.broadcast_to(bundle.reshape(1, 9, 1, members), (128, 9, 1, members))
    arrived = lax.all_to_all(bundle, ("gx", "gy"), 0, 0, tiled=True)

    state = pl.pallas_call(
        forecast_kernel,
        out_shape=jax.ShapeDtypeStruct(cells.shape, F32),
        in_specs=[hbm()] + [vmem()] * 3 + [hbm()] * 2 + [vmem()] * 6,
        out_specs=vmem(),
        scratch_shapes=[
            pltpu.VMEM((4, 3, CY, 128), F32),
            pltpu.VMEM((COMP, CX + 4, CY + 16, MEM), F32),
            pltpu.VMEM((2, CX + 4, CY + 16, MEM), F32),
            pltpu.SemaphoreType.DMA((4,)),
        ],
        compiler_params=pltpu.CompilerParams(vmem_limit_bytes=32 << 20),
        name="forecast",
    )(cells, *speeds, halo_w, halo_e, halo_s, halo_n, from_west, from_east, from_south, from_north)
    state = state.reshape(-1, members)

    result = analyse(
        pos, counts, arrived.reshape(-1, members), slots, perm, source, place, obs_weight, select, state
    )
    return result.reshape(comps, zonal_extent, width_y, members)


def solution(mesh):
    return jax.shard_map(
        shards,
        mesh=mesh,
        in_specs=(
            P(None, "gx", "gy", None),
            P(None, "gx", "gy"),
            P(None, "gx", "gy"),
            P(None, "gx", "gy"),
            P(),
            P(),
            P(),
            P(),
            P(),
            P("gx", "gy", None),
            P("gx", "gy", None),
        ),
        out_specs=P(None, "gx", "gy", None),
        check_vma=False,
    )
```

```python
import jax
import jax.numpy as jnp
from jax import lax
from jax.experimental import pallas as pl
from jax.experimental.pallas import tpu as pltpu
from jax.sharding import PartitionSpec as P

FSTEPS = 2
PANEL = 256
PANELS = 4
NOBS = 1024
COMP = 8
CX = 16
CY = 32
MEM = 128
BLOCK = CX * CY
F32 = jnp.float32
BF16 = jnp.bfloat16
NT = (((1,), (1,)), ((), ()))
NN = (((1,), (0,)), ((), ()))


def dot(left, right, dims=NN):
    return lax.dot_general(left, right, dims, preferred_element_type=F32)


def halves(full):
    high = full.astype(BF16)
    low = (full - high.astype(F32)).astype(BF16)
    return high, low


def as_columns(row):
    return jnp.transpose(jnp.broadcast_to(row, (128, row.shape[1])))


def plan_kernel(pos, table, perm, obs_weight, select, slots, source, place, counts):
    here_x = pos[0]
    here_y = pos[1]
    owner = table[4:5, :]
    lane = lax.broadcasted_iota(jnp.int32, (1, NOBS), 1)
    within = lane & 7
    rank = jnp.zeros((1, NOBS), jnp.int32)
    for gap in range(1, 8):
        same = (within >= gap) & (pltpu.roll(owner, gap, 1) == owner)
        rank = rank + same.astype(jnp.int32)
    place_row = (lane >> 6) * 2 + rank
    source_row = owner * 8 + ((lane >> 3) & 7)
    facts = jnp.concatenate(
        [table[0:4, :], place_row, source_row, jnp.zeros((2, NOBS), jnp.int32)], axis=0
    ).astype(F32)
    order = as_columns(table[5:6, :].astype(F32))
    lanes = lax.broadcasted_iota(jnp.int32, (NOBS, 128), 1).astype(F32)
    for part in range(NOBS // 128):
        hit = order == lanes + float(128 * part)
        perm[:, part * 128 : (part + 1) * 128] = jnp.where(hit, 1.0, 0.0).astype(BF16)
    ordered = dot(facts.astype(BF16), perm[...], NT)

    col_x = as_columns(ordered[0:1])
    col_y = as_columns(ordered[1:2])
    col_l = as_columns(ordered[2:3])
    place[...] = as_columns(ordered[4:5])
    col_s = as_columns(ordered[5:6])
    source[...] = jnp.where(col_s == lanes, 1.0, 0.0).astype(BF16)
    inverse = 1.0 / (ordered[3:4] + 1.0)
    first = 0
    for panel in range(PANELS - 1):
        begin = (panel + 1) * PANEL
        rows = NOBS - begin
        for part in range(PANEL // 128):
            cols = slice(panel * PANEL + part * 128, panel * PANEL + (part + 1) * 128)
            gap_x = jnp.abs(col_x[begin:] - ordered[0:1, cols])
            gap_x = jnp.minimum(gap_x, 256.0 - gap_x)
            gap_y = col_y[begin:] - ordered[1:2, cols]
            near = jnp.maximum(0.0, 1.0 - (gap_x * gap_x * (1.0 / 2304.0) + gap_y * gap_y * (1.0 / 9216.0)))
            gap_l = jnp.abs(col_l[begin:] - ordered[2:3, cols])
            level = jnp.maximum(0.0, 1.0 - gap_l * inverse[:, cols])
            obs_weight[first : first + rows, part * 128 : (part + 1) * 128] = (
                near * near * level * (1.0 / (MEM - 1))
            )
        first += rows

    whole = ordered.astype(jnp.int32)
    off_x = (whole[0:1] - here_x * CX) & 255
    far_x = jnp.where(off_x < CX, 0, jnp.minimum(off_x - (CX - 1), 256 - off_x))
    off_y = whole[1:2] - here_y * CY
    far_y = jnp.maximum(0, jnp.maximum(-off_y, off_y - (CY - 1)))
    reached = jnp.where(4 * far_x * far_x + far_y * far_y < 9216, 1.0, 0.0)
    before = lax.broadcasted_iota(jnp.int32, (PANEL, PANEL), 0) < lax.broadcasted_iota(
        jnp.int32, (PANEL, PANEL), 1
    )
    before = jnp.where(before, 1.0, 0.0).astype(BF16)
    slot = lax.broadcasted_iota(jnp.int32, (PANEL, PANEL), 0).astype(F32)
    for panel in range(PANELS):
        cols = slice(panel * PANEL, (panel + 1) * PANEL)
        mask = reached[:, cols]
        ranks = dot(jnp.broadcast_to(mask, (8, PANEL)).astype(BF16), before)[0:1]
        chosen = jnp.where((slot == ranks) & (mask > 0.0), 1.0, 0.0).astype(BF16)
        select[panel] = chosen
        packed = dot(ordered[:, cols].astype(BF16), chosen, NT)
        slots[panel] = jnp.concatenate(
            [packed[0:3], 1.0 / (packed[3:4] + 1.0), packed[4:8]], axis=0
        )
        counts[panel] = jnp.sum(mask).astype(jnp.int32)


def analysis_kernel(
    pos, counts, arrived, slots, perm_far, source_far, place_far, weight_far, select_far, state_far,
    out, rows, near, left, right, perm, source, place, obs_weight, select, state, arrivals,
):
    here_x = pos[0]
    here_y = pos[1]
    copies = [
        pltpu.make_async_copy(far, close, arrivals.at[index])
        for index, (far, close) in enumerate(
            (
                (perm_far, perm),
                (source_far, source),
                (place_far, place),
                (weight_far, obs_weight),
                (select_far, select),
                (state_far, state),
            )
        )
    ]
    for copy in copies:
        copy.start()
    for k in range(8):
        rows[pl.ds(k, 128, stride=8), :] = arrived[pl.ds(k, 128, stride=9), :]
    given = arrived[pl.ds(8, 128, stride=9), :]
    high, low = halves(rows[...])
    both = jnp.concatenate([high, low], axis=1)
    copies[0].wait()
    for panel in range(PANELS):
        span = slice(panel * PANEL, (panel + 1) * PANEL)
        moved = dot(perm[span, :], both)
        rows[span, :] = moved[:, :MEM] + moved[:, MEM:]
    v_high = given.astype(BF16)
    rest = given - v_high.astype(F32)
    v_mid = rest.astype(BF16)
    v_low = (rest - v_mid.astype(F32)).astype(BF16)
    v_all = jnp.concatenate([v_high, v_mid, v_low], axis=1)
    lanes = lax.broadcasted_iota(jnp.int32, (PANEL, 128), 1).astype(F32)

    copies[1].wait()
    copies[2].wait()
    first = 0
    for panel in range(PANELS):
        span = slice(panel * PANEL, (panel + 1) * PANEL)
        held = dot(source[span, :], v_all)
        held = held[:, :128] + held[:, 128:256] + held[:, 256:]
        here = place[span, :]
        value = jnp.sum(jnp.where(lanes == here, held, 0.0), axis=1, keepdims=True)
        error = jnp.sum(jnp.where(lanes == here + 32.0, held, 0.0), axis=1, keepdims=True)
        prior = rows[span, :]
        centre = jnp.sum(prior, axis=1, keepdims=True) * (1.0 / MEM)
        spread = prior - centre
        variance = jnp.sum(spread * spread, axis=1, keepdims=True) / (MEM - 1)
        inverse = 1.0 / (variance + error)
        gain = (value - centre) * inverse
        shrink = inverse / (1.0 + jnp.sqrt(error * inverse))
        change = gain - shrink * spread
        q_high, q_low = halves(spread)
        h_high, h_low = halves(change)
        if panel < PANELS - 1:
            begin = (panel + 1) * PANEL
            count = NOBS - begin
            later = rows[begin:, :]
            l_high, l_low = halves(later - jnp.sum(later, axis=1, keepdims=True) * (1.0 / MEM))
            q_both = jnp.concatenate(
                [jnp.concatenate([q_high, q_high], axis=1), jnp.concatenate([q_low, q_low], axis=1)], axis=0
            )
            cov = dot(jnp.concatenate([l_high, l_low], axis=1), q_both, NT)
            if panel == 0:
                copies[3].wait()
            local = (cov[:, :PANEL] + cov[:, PANEL:]) * obs_weight[first : first + count, :]
            g_high, g_low = halves(local)
            h_both = jnp.concatenate([h_high, h_low], axis=1)
            step = dot(g_high, h_both) + dot(g_low, h_both)
            rows[begin:, :] = later + (step[:, :MEM] + step[:, MEM:])
            first += count
        if panel == 0:
            copies[4].wait()
        packed = dot(select[panel], jnp.concatenate([q_high, q_low, h_high, h_low], axis=1)).astype(BF16)
        for part in range(2):
            half = packed[part * 128 : (part + 1) * 128]
            q_h, q_l, h_h, h_l = (half[:, i * MEM : (i + 1) * MEM] for i in range(4))
            left[panel, part] = jnp.concatenate(
                [jnp.concatenate([q_h, q_h], axis=1), jnp.concatenate([q_l, q_l], axis=1)], axis=0
            )
            h_row = jnp.concatenate([h_h, h_l], axis=1)
            right[panel, part] = jnp.concatenate([h_row, h_row], axis=0)
        fact = slots[panel]
        step_x = lax.broadcasted_iota(jnp.int32, (CX, PANEL), 0) + here_x * CX
        gap_x = jnp.abs(step_x.astype(F32) - fact[0:1])
        gap_x = jnp.minimum(gap_x, 256.0 - gap_x)
        part_x = 1.0 - gap_x * gap_x * (1.0 / 2304.0)
        step_y = lax.broadcasted_iota(jnp.int32, (CY, PANEL), 0) + here_y * CY
        gap_y = step_y.astype(F32) - fact[1:2]
        part_y = gap_y * gap_y * (1.0 / 9216.0)
        for col in range(CX):
            close = jnp.maximum(0.0, part_x[col : col + 1] - part_y)
            near[panel, col * CY : (col + 1) * CY, :] = close * close * (1.0 / (MEM - 1))

    copies[5].wait()

    @pl.loop(0, COMP)
    def _(comp):
        level = (comp // 2).astype(F32)
        at = pl.ds(pl.multiple_of(comp * BLOCK, BLOCK), BLOCK)
        block = state[at, :]
        mean = jnp.sum(block, axis=1, keepdims=True) * (1.0 / MEM)
        out[at, :] = block - mean
        for panel in range(PANELS):
            fact = slots[panel]
            level_weight = jnp.maximum(0.0, 1.0 - jnp.abs(fact[2:3] - level) * fact[3:4])

            def local_step(both, part):
                cov = dot(both, left[panel, part], NT)
                cols = slice(part * 128, (part + 1) * 128)
                local = (cov[:, :128] + cov[:, 128:]) * (near[panel, :, cols] * level_weight[:, cols])
                g_high, g_low = halves(local)
                step = dot(jnp.concatenate([g_high, g_low], axis=1), right[panel, part])
                return step[:, :MEM] + step[:, MEM:]

            old = out[at, :]
            old_high, old_low = halves(old)
            old_both = jnp.concatenate([old_high, old_low], axis=1)
            out[at, :] = old + local_step(old_both, 0)

            @pl.when(counts[panel] > 128)
            def _():
                out[at, :] = out[at, :] + local_step(old_both, 1)
        out[at, :] = out[at, :] + mean


OFFSETS = (
    (0, 0), (-1, 0), (1, 0), (0, -1), (0, 1),
    (-1, -1), (-1, 1), (1, -1), (1, 1),
    (-2, 0), (2, 0), (0, -2), (0, 2),
)


def edge_kernel(pos, code, cells, east, north, diff, own, own_coef, to_east, to_west, to_north, to_south):
    here_x = pos[0]
    here_y = pos[1]
    coefs = (east, north, diff)

    def look(shift_x, shift_y, k):
        tile_x = (here_x + shift_x) & 15
        tile_y = jnp.clip(here_y + shift_y, 0, 7)
        word = code[(tile_x * 8 + tile_y) * 8 + k]
        return word & 15, (word >> 8) & 31, word >> 16

    def cell(comp, x, y):
        return cells[pl.ds((comp * CX + x) * CY + y, 1), :]

    def clip_x(x):
        return jnp.clip(x, 0, CX - 1)

    def clip_y(y):
        return jnp.clip(y, 0, CY - 1)

    for k in range(8):
        x, y, comp = look(0, 0, k)
        for index, (step_x, step_y) in enumerate(OFFSETS):
            at = index * 8 + k
            own[at : at + 1, :] = cell(comp, clip_x(x + step_x), clip_y(y + step_y))
        for step_x in (-1, 0, 1):
            for c in range(3):
                at = (c * 3 + step_x + 1) * 8 + k
                own_coef[at : at + 1, 0:CY] = coefs[c][pl.ds((comp >> 1) * CX + clip_x(x + step_x), 1), :]
        for shift, target, edge in ((1, to_east, CX - 1), (-1, to_west, 0)):
            x, y, comp = look(shift, 0, k)
            for index, step_y in enumerate((-1, 0, 1)):
                at = index * 8 + k
                target[at : at + 1, :] = cell(comp, edge, clip_y(y + step_y))
            target[24 + k : 25 + k, :] = cell(comp, clip_x(x + shift * (CX - 2)), y)
            _, _, comp = look(shift, 1, k)
            target[32 + k : 33 + k, :] = cell(comp, edge, CY - 1)
            _, _, comp = look(shift, -1, k)
            target[40 + k : 41 + k, :] = cell(comp, edge, 0)
        for shift, target, edge in ((1, to_north, CY - 1), (-1, to_south, 0)):
            x, y, comp = look(0, shift, k)
            for index, step_x in enumerate((-1, 0, 1)):
                at = index * 8 + k
                target[at : at + 1, :] = cell(comp, clip_x(x + step_x), edge)
            target[24 + k : 25 + k, :] = cell(comp, x, clip_y(y + shift * (CY - 2)))
    for target, edge in ((to_east, CX - 1), (to_west, 0)):
        target[48:64, :] = jnp.zeros((16, MEM), F32)
        for comp in range(COMP):
            target[64 + comp : 65 + comp, :] = cell(comp, edge, CY - 1)
            target[72 + comp : 73 + comp, :] = cell(comp, edge, 0)
        for c in range(3):
            for level in range(4):
                at = 48 + c * 4 + level
                target[at : at + 1, 0:CY] = coefs[c][level * CX + edge : level * CX + edge + 1, :]
    lanes = lax.broadcasted_iota(jnp.int32, (CX, MEM), 1)
    for target, edge in ((to_north, CY - 1), (to_south, 0)):
        table = jnp.zeros((CX, MEM), F32)
        for c in range(3):
            for level in range(4):
                line = coefs[c][level * CX : (level + 1) * CX, edge : edge + 1]
                table = jnp.where(lanes == c * 4 + level, line, table)
        target[32:48, :] = table


def obs_columns(pos, code):
    begin = (pos[0] * 8 + pos[1]) * 8
    row = lax.broadcasted_iota(jnp.int32, (8, MEM), 0)
    word = jnp.zeros((8, MEM), jnp.int32)
    for k in range(8):
        word = jnp.where(row == k, code[begin + k], word)
    return word & 15, (word >> 8) & 31, word >> 16


def corner_kernel(pos, code, base_north, base_south, from_west, from_east, to_north, to_south):
    row = lax.broadcasted_iota(jnp.int32, (8, MEM), 0)
    for shift, base, target, first in ((1, base_north, to_north, 32), (-1, base_south, to_south, 40)):
        tile_y = jnp.clip(pos[1] + shift, 0, 7)
        begin = (pos[0] * 8 + tile_y) * 8
        x = jnp.zeros((8, MEM), jnp.int32)
        for k in range(8):
            x = jnp.where(row == k, code[begin + k] & 15, x)
        target[0:48, :] = base[...]
        corners = 64 if shift == 1 else 72
        target[48:56, :] = from_west[corners : corners + 8, :]
        target[56:64, :] = from_east[corners : corners + 8, :]
        target[0:8, :] = jnp.where(x == 0, from_west[first : first + 8, :], base[0:8, :])
        target[16:24, :] = jnp.where(x == CX - 1, from_east[first : first + 8, :], base[16:24, :])


def prior_kernel(
    pos, code, own, own_coef, from_west, from_east, from_south, from_north, held, out, scratch
):
    x, y, comp = obs_columns(pos, code)
    level = comp >> 1
    west = x == 0
    east = x == CX - 1
    begin = (pos[0] * 8 + pos[1]) * 8
    for k in range(8):
        word = code[begin + k]
        here_l = word >> 17
        for c in range(3):
            at = c * 8 + k
            scratch[at : at + 1, :] = from_west[pl.ds(48 + c * 4 + here_l, 1), :]
            scratch[24 + at : 25 + at, :] = from_east[pl.ds(48 + c * 4 + here_l, 1), :]
        scratch[48 + k : 49 + k, :] = from_south[pl.ds(32 + (word & 15), 1), :]
        scratch[56 + k : 57 + k, :] = from_north[pl.ds(32 + (word & 15), 1), :]

    state = {}
    for index, (step_x, step_y) in enumerate(OFFSETS):
        value = own[index * 8 : index * 8 + 8, :]
        if step_x < 0:
            group = 3 if step_x == -2 else step_y + 1
            value = jnp.where(x + step_x < 0, from_west[group * 8 : group * 8 + 8, :], value)
        if step_x > 0:
            group = 3 if step_x == 2 else step_y + 1
            value = jnp.where(x + step_x >= CX, from_east[group * 8 : group * 8 + 8, :], value)
        if step_y < 0:
            group = 3 if step_y == -2 else step_x + 1
            value = jnp.where(y + step_y < 0, from_south[group * 8 : group * 8 + 8, :], value)
        if step_y > 0:
            group = 3 if step_y == 2 else step_x + 1
            value = jnp.where(y + step_y >= CY, from_north[group * 8 : group * 8 + 8, :], value)
        state[(step_x, step_y)] = value

    lanes = lax.broadcasted_iota(jnp.int32, (8, MEM), 1)
    at_y = lanes[:, :CY] - y[:, :CY]

    def pick(values, mask):
        return jnp.sum(jnp.where(mask, values, 0.0), axis=1, keepdims=True)

    def rows_of(c, step_x):
        at = (c * 3 + step_x + 1) * 8
        return own_coef[at : at + 8, 0:CY]

    def coefs_at(step_x, step_y):
        found = []
        for c in range(3):
            value = pick(rows_of(c, step_x), at_y == step_y)
            if step_x == -1:
                value = jnp.where(west[:, :1], pick(scratch[c * 8 : c * 8 + 8, 0:CY], at_y == 0), value)
            if step_x == 1:
                value = jnp.where(east[:, :1], pick(scratch[24 + c * 8 : 32 + c * 8, 0:CY], at_y == 0), value)
            mine = lanes == c * 4 + level
            if step_y == -1:
                value = jnp.where(y[:, :1] == 0, pick(scratch[48:56, :], mine), value)
            if step_y == 1:
                value = jnp.where(y[:, :1] == CY - 1, pick(scratch[56:64, :], mine), value)
            found.append(value)
        return found

    def advance(field, step_x, step_y):
        u, v, nu = coefs_at(step_x, step_y)
        mid = field[(step_x, step_y)]
        e = field[(step_x + 1, step_y)]
        w = field[(step_x - 1, step_y)]
        n = field[(step_x, step_y + 1)]
        s = field[(step_x, step_y - 1)]
        return mid + nu * (e + w + n + s - 4.0 * mid) - 0.5 * (u * (e - w) + v * (n - s))

    after = {key: advance(state, *key) for key in OFFSETS[:5]}
    out[0:8, :] = advance(after, 0, 0)
    out[8:9, :] = held[...]


def stencil(mid, e, w, n, s, u, v, nu):
    return mid + nu * (e + w + n + s - 4.0 * mid) - 0.5 * (u * (e - w) + v * (n - s))


def forecast_kernel(
    cells, east, north, diff, halo_w, halo_e, halo_s, halo_n, edge_w, edge_e, edge_s, edge_n,
    out, table, before, after, arrivals,
):
    rows = pl.ds(8, CY)
    copies = []
    for level in range(4):
        pair = pl.ds(level * 2, 2)
        copies.append(
            [
                pltpu.make_async_copy(far.at[pair], before.at[pair, cols, rows, :], arrivals.at[level])
                for far, cols in ((cells, pl.ds(2, CX)), (halo_w, pl.ds(0, 2)), (halo_e, pl.ds(2 + CX, 2)))
            ]
        )
        for copy in copies[level]:
            copy.start()
    coefs = (east, north, diff)
    pad = jnp.zeros((128 - CX, CY), F32)
    fill = jnp.zeros((128, 128 - CY), F32)
    for c in range(3):
        for level in range(4):
            tile = coefs[c][level * CX : (level + 1) * CX, :]
            ends = jnp.concatenate(
                [
                    tile,
                    edge_w[48 + c * 4 + level : 49 + c * 4 + level, 0:CY],
                    edge_e[48 + c * 4 + level : 49 + c * 4 + level, 0:CY],
                    pad[: 128 - CX - 2],
                ],
                axis=0,
            )
            turned = jnp.transpose(jnp.concatenate([ends, fill], axis=1))
            table[level, c] = turned[0:CY, :]

    mid_rows = slice(8, 8 + CY)
    for level in range(4):
        for copy in copies[level]:
            copy.wait()
        for which in range(2):
            comp = level * 2 + which
            for rim, edge, inner, target in ((halo_s, edge_s, 1, 7), (halo_n, edge_n, 0, 8 + CY)):
                before[level * 2 + which, 2 : 2 + CX, target, :] = rim[comp, :, inner, :]
                before[level * 2 + which, 1, target : target + 1, :] = edge[48 + comp : 49 + comp, :]
                before[level * 2 + which, 2 + CX, target : target + 1, :] = edge[56 + comp : 57 + comp, :]
        for col in range(-1, CX + 1):
            lane = CX if col < 0 else (CX + 1 if col == CX else col)
            u, v, nu = (
                jnp.broadcast_to(table[level, c, :, lane : lane + 1], (CY, MEM)) for c in range(3)
            )
            at = col + 2
            for which in range(2):
                after[which, at, mid_rows, :] = stencil(
                    before[level * 2 + which, at, mid_rows, :],
                    before[level * 2 + which, at + 1, mid_rows, :],
                    before[level * 2 + which, at - 1, mid_rows, :],
                    before[level * 2 + which, at, 9 : 9 + CY, :],
                    before[level * 2 + which, at, 7 : 7 + CY, :],
                    u, v, nu,
                )
        for rim, edge, outer, inside, target in (
            (halo_s, edge_s, 0, 0, 7),
            (halo_n, edge_n, 1, CY - 1, 8 + CY),
        ):
            u, v, nu = (
                jnp.broadcast_to(edge[32:48, c * 4 + level : c * 4 + level + 1], (CX, MEM))
                for c in range(3)
            )
            for which in range(2):
                comp = level * 2 + which
                mid = before[level * 2 + which, 2 : 2 + CX, target, :]
                e = before[level * 2 + which, 3 : 3 + CX, target, :]
                w = before[level * 2 + which, 1 : 1 + CX, target, :]
                far = rim[comp, :, outer, :]
                close = before[comp, 2 : 2 + CX, 8 + inside, :]
                n, s = (close, far) if target == 7 else (far, close)
                after[which, 2 : 2 + CX, target, :] = stencil(mid, e, w, n, s, u, v, nu)
        for col in range(CX):
            u, v, nu = (
                jnp.broadcast_to(table[level, c, :, col : col + 1], (CY, MEM)) for c in range(3)
            )
            at = col + 2
            for which in range(2):
                out[level * 2 + which, col] = stencil(
                    after[which, at, mid_rows, :],
                    after[which, at + 1, mid_rows, :],
                    after[which, at - 1, mid_rows, :],
                    after[which, at, 9 : 9 + CY, :],
                    after[which, at, 7 : 7 + CY, :],
                    u, v, nu,
                )


def vmem():
    return pl.BlockSpec(memory_space=pltpu.VMEM)


def hbm():
    return pl.BlockSpec(memory_space=pltpu.HBM)


def smem():
    return pl.BlockSpec(memory_space=pltpu.SMEM)


def plan(pos, table):
    shapes = (
        jax.ShapeDtypeStruct((NOBS, NOBS), BF16),
        jax.ShapeDtypeStruct((6 * PANEL, PANEL), F32),
        jax.ShapeDtypeStruct((PANELS, PANEL, PANEL), BF16),
        jax.ShapeDtypeStruct((PANELS, 8, PANEL), F32),
        jax.ShapeDtypeStruct((NOBS, 128), BF16),
        jax.ShapeDtypeStruct((NOBS, 128), F32),
        jax.ShapeDtypeStruct((PANELS,), jnp.int32),
    )
    return pl.pallas_call(
        plan_kernel,
        out_shape=shapes,
        in_specs=[smem(), vmem()],
        out_specs=[vmem()] * 6 + [smem()],
        name="plan",
    )(pos, table)


def analyse(pos, counts, arrived, slots, *far):
    return pl.pallas_call(
        analysis_kernel,
        out_shape=jax.ShapeDtypeStruct(far[-1].shape, F32),
        in_specs=[smem(), smem(), vmem(), vmem()] + [hbm()] * len(far),
        out_specs=vmem(),
        scratch_shapes=[
            pltpu.VMEM((NOBS, MEM), F32),
            pltpu.VMEM((PANELS, BLOCK, PANEL), F32),
            pltpu.VMEM((PANELS, 2, PANEL, PANEL), BF16),
            pltpu.VMEM((PANELS, 2, PANEL, PANEL), BF16),
        ]
        + [pltpu.VMEM(array.shape, array.dtype) for array in far]
        + [pltpu.SemaphoreType.DMA((len(far),))],
        compiler_params=pltpu.CompilerParams(vmem_limit_bytes=62 << 20),
        name="analyse",
    )(pos, counts, arrived, slots, *far)


def shards(
    prior_member_matrix,
    east_speed,
    north_speed,
    diffusion,
    obs_column,
    obs_comp,
    observation_reach,
    obs_owner,
    obs_order,
    obs_value,
    obs_error,
):
    comps, zonal_extent, width_y, members = prior_member_matrix.shape
    per_level = comps // east_speed.shape[0]
    here_x = lax.axis_index("gx")
    here_y = lax.axis_index("gy")
    pos = jnp.stack([here_x, here_y]).astype(jnp.int32)
    zero = jnp.zeros_like(obs_comp)
    table = jnp.stack(
        [
            obs_column[:, 0],
            obs_column[:, 1],
            obs_comp // per_level,
            observation_reach,
            obs_owner,
            obs_order,
            zero,
            zero,
        ]
    )

    def rows(count, width=MEM):
        return jax.ShapeDtypeStruct((count, width), F32)

    def along_x(value, step):
        return lax.ppermute(value, "gx", [(i, (i + step) % 16) for i in range(16)])

    def along_y(value, step):
        return lax.ppermute(value, "gy", [(i, i + step) for i in range(8) if 0 <= i + step < 8])

    code = obs_column[:, 0] + obs_column[:, 1] * 256 + obs_comp * 65536
    cells = prior_member_matrix
    flat = cells.reshape(-1, members)
    speeds = [field.reshape(-1, width_y) for field in (east_speed, north_speed, diffusion)]
    own, own_coef, to_east, to_west, base_north, base_south = pl.pallas_call(
        edge_kernel,
        out_shape=(rows(104), rows(72), rows(80), rows(80), rows(48), rows(48)),
        in_specs=[smem(), smem()] + [vmem()] * 4,
        out_specs=[vmem()] * 6,
        name="edges",
    )(pos, code, flat, *speeds)
    from_west = along_x(to_east, 1)
    from_east = along_x(to_west, -1)
    from_west, from_east, late = lax.optimization_barrier((from_west, from_east, cells))
    halo_w = along_x(late[:, CX - 2 :], 1)
    halo_e = along_x(late[:, :2], -1)
    halo_s = along_y(late[:, :, CY - 2 :], 1)
    halo_n = along_y(late[:, :, :2], -1)
    to_north, to_south = pl.pallas_call(
        corner_kernel,
        out_shape=(rows(64), rows(64)),
        in_specs=[smem(), smem()] + [vmem()] * 4,
        out_specs=[vmem()] * 2,
        name="corners",
    )(pos, code, base_north, base_south, from_west, from_east)
    from_south = along_y(to_north, 1)
    from_north = along_y(to_south, -1)
    held = jnp.concatenate([obs_value.reshape(1, -1), obs_error.reshape(1, -1)], axis=1)
    held = jnp.pad(held, ((0, 0), (0, members - held.shape[1])))
    bundle = pl.pallas_call(
        prior_kernel,
        out_shape=rows(9),
        in_specs=[smem(), smem()] + [vmem()] * 7,
        out_specs=vmem(),
        scratch_shapes=[pltpu.VMEM((64, MEM), F32)],
        name="priors",
    )(pos, code, own, own_coef, from_west, from_east, from_south, from_north, held)

    bundle, table = lax.optimization_barrier((bundle, table))
    perm, obs_weight, select, slots, source, place, counts = plan(pos, table)
    bundle = jnp.broadcast_to(bundle.reshape(1, 9, 1, members), (128, 9, 1, members))
    arrived = lax.all_to_all(bundle, ("gx", "gy"), 0, 0, tiled=True)

    state = pl.pallas_call(
        forecast_kernel,
        out_shape=jax.ShapeDtypeStruct(cells.shape, F32),
        in_specs=[hbm()] + [vmem()] * 3 + [hbm()] * 2 + [vmem()] * 6,
        out_specs=vmem(),
        scratch_shapes=[
            pltpu.VMEM((4, 3, CY, 128), F32),
            pltpu.VMEM((COMP, CX + 4, CY + 16, MEM), F32),
            pltpu.VMEM((2, CX + 4, CY + 16, MEM), F32),
            pltpu.SemaphoreType.DMA((4,)),
        ],
        compiler_params=pltpu.CompilerParams(vmem_limit_bytes=62 << 20),
        name="forecast",
    )(cells, *speeds, halo_w, halo_e, halo_s, halo_n, from_west, from_east, from_south, from_north)
    state = state.reshape(-1, members)

    result = analyse(
        pos, counts, arrived.reshape(-1, members), slots, perm, source, place, obs_weight, select, state
    )
    return result.reshape(comps, zonal_extent, width_y, members)


def solution(mesh):
    return jax.shard_map(
        shards,
        mesh=mesh,
        in_specs=(
            P(None, "gx", "gy", None),
            P(None, "gx", "gy"),
            P(None, "gx", "gy"),
            P(None, "gx", "gy"),
            P(),
            P(),
            P(),
            P(),
            P(),
            P("gx", "gy", None),
            P("gx", "gy", None),
        ),
        out_specs=P(None, "gx", "gy", None),
        check_vma=False,
    )
```
